32 devices in a mesh: dp: 4 (over y, x), fsdp: 8 (over z, core).
Axes of the slice: x: 2, y: 2, z: 4, core: 2. Of those that a mesh axis runs over, the one named last changes fastest.
Arguments:
- inputs: bfloat16 [512, 16384], P('dp', 'fsdp'), may hold values from -140 to 140
- norm_gain_vector: bfloat16 [16384], P('fsdp'), may hold values from 0.5 to 1.5
- weight: bfloat16 [16384, 16384], P(None, 'fsdp'), may hold values from -0.046875 to 0.046875
- down_adapters: bfloat16 [16384, 16, 32], P('fsdp'), may hold values from -0.046875 to 0.046875
- up_adapters: bfloat16 [16, 32, 16384], P(None, None, 'fsdp'), may hold values from -1 to 1
- tenant: int32 [512], P('dp'), may hold values from 0 to 15
- tenant_slot_index: int32 [16], replicated, may hold values from 0 to 31, as said below
- live_row_count: int32 [4], P('dp'), may hold values from 1 to 128, 320 in all
- cotangent: bfloat16 [512, 16384], P('dp', 'fsdp'), may hold values from -6 to 6
- down_row_factor: float32 [32, 16384], P('dp', 'fsdp'), may hold values from 300 to 30000
- down_column_factor: float32 [32, 32], P('dp'), may hold values from 300 to 30000
- up_row_factor: float32 [32, 32], P('dp'), may hold values from 0.5 to 50
- up_column_factor: float32 [32, 16384], P('dp', 'fsdp'), may hold values from 0.5 to 50
Outputs:
- projected: bfloat16 [512, 16384], P('dp', 'fsdp')
- normed_gradient_transposed: bfloat16 [16384, 512], P('fsdp', 'dp')
- update_a: float32 [32, 16384, 32], P('dp', 'fsdp')
- update_b: float32 [32, 32, 16384], P('dp', None, 'fsdp')
- row_a_new: float32 [32, 16384], P('dp', 'fsdp')
- col_a_new: float32 [32, 32], P('dp')
- row_b_new: float32 [32, 32], P('dp')
- col_b_new: float32 [32, 16384], P('dp', 'fsdp')
The draws below stay inside these ranges and needn't reach their ends.
Inputs may be any that keep to these rules, and one draw needn't show every extreme that they name: Distinct slots; tenant t's optimizer state is in slot tenant_slot_index[t], owned by data group tenant_slot_index[t] // 8; every group owns at most 8 tenants and some group owns exactly 8. The first live_row_count[g] rows of data group g are live; some group has all 128 live; the counts sum to 320.
All inputs are finite; a program needn't handle non-finite values.
Results may differ from the reference program's by a relative error of at most 0.0095.
Values may be sent and summed in bfloat16 or wider, within the bound.
A program may use at most 192 MiB of HBM per device.

```python
import math
import jax
import jax.numpy as jnp
import numpy as np
from jax import lax

MODEL_WIDTH = 16384
ADAPTER_RANK = 32
TENANT_COUNT = 16
CAP = 8
ROWS = 128
ROWS_ALL = 512
SLOTS = 32
N_DP = 4


def draw_inputs(key, part):
    key_base, key_cols, key_rows = jax.random.split(jax.random.fold_in(key, 11), 3)
    position = jnp.arange(MODEL_WIDTH, dtype=jnp.float32) / MODEL_WIDTH
    columns = jnp.exp(jnp.log(3.0) * position) * jnp.exp(jax.random.uniform(key_cols, (MODEL_WIDTH,), jnp.float32, 0.0, 1.2))
    rowscale = jnp.exp(jax.random.uniform(key_rows, (ROWS_ALL, 1), jnp.float32, 0.0, jnp.log(10.0)))
    frozen_output = jnp.clip(jax.random.normal(key_base, (ROWS_ALL, MODEL_WIDTH), jnp.float32), -4.0, 4.0)
    return (frozen_output * columns[None, :] * rowscale / 3.0).astype(jnp.bfloat16)


def draw_tenant_slot_index(key, part):
    key_full, key_order, key_other = jax.random.split(jax.random.fold_in(key, 23), 3)
    full = jax.random.randint(key_full, (), 0, N_DP)
    order = jax.random.permutation(key_order, TENANT_COUNT)
    others = jax.random.permutation(key_other, (N_DP - 1) * CAP)
    group = others // CAP
    group = group + (group >= full).astype(jnp.int32)
    other_slots = (group * CAP + others % CAP).astype(jnp.int32)
    filler = jnp.concatenate([jnp.zeros((CAP,), jnp.int32), other_slots[:TENANT_COUNT - CAP]])
    ranked = jnp.arange(TENANT_COUNT, dtype=jnp.int32)
    slot_by_rank = jnp.where(ranked < CAP, full * CAP + ranked, filler).astype(jnp.int32)
    return jnp.zeros((TENANT_COUNT,), jnp.int32).at[order].set(slot_by_rank)


def set_ends(result, stream_key, low, largest):
    longest = result.shape.index(max(result.shape))
    spots = []
    for shift in (0, 1):
        where = [jax.random.randint(jax.random.fold_in(stream_key, axis), (), 0, length) for axis, length in enumerate(result.shape)]
        where[longest] = (where[longest] + shift) % result.shape[longest]
        spots.append(tuple(where))
    return result.at[spots[0]].set(low).at[spots[1]].set(largest)


def block_scale(stream_key, dims, cuts, smallest, largest):
    factor_of, own = 1.0, jax.random.fold_in(stream_key, 6)
    for axis_at, blocks in cuts:
        steps = jnp.exp(jax.random.uniform(jax.random.fold_in(own, axis_at), (blocks,), jnp.float32, smallest / len(cuts), largest / len(cuts)))
        factor_of = factor_of * jnp.repeat(steps, dims[axis_at] // blocks).reshape([-1 if axis == axis_at else 1 for axis in range(len(dims))])
    return factor_of


def cumulative_ranks(count, lean):
    loads = [(1 << 20) // math.isqrt(rank ** lean) + 1 for rank in range(1, count + 1)]
    width = 1 + sum(loads) // (1 << 30)
    return np.cumsum(np.array([max(1, weight // width) for weight in loads]))


def skewed_ids(stream_key, dims, number_of, lean):
    table = cumulative_ranks(number_of, lean)
    ticket = jax.random.randint(jax.random.fold_in(stream_key, 1), dims, 0, int(table[number_of - 1]))
    rank = jnp.searchsorted(jnp.asarray(table, jnp.int32), ticket, side="right")
    return jax.random.permutation(jax.random.fold_in(stream_key, 2), number_of)[rank].astype(jnp.int32)


def split_up(number_of, total, most, lean):
    loads = [(1 << 20) // math.isqrt(standing ** lean) + 1 for standing in range(2, number_of + 1)]
    spare, counts = total - most - (number_of - 1), [1] * (number_of - 1)
    while spare > 0:
        candidates = [i for i in range(number_of - 1) if counts[i] < most]
        pool, budget = sum([loads[i] for i in candidates]), spare
        for i in candidates:
            addition = min(most - counts[i], max(1, budget * loads[i] // pool), spare)
            counts[i] = counts[i] + addition
            spare = spare - addition
    return np.array([most] + counts)


def uneven(rng, number_of, total, bound, slope):
    if number_of == 2:
        one = jax.random.randint(rng, (), max(1, total - bound), min(bound, total - 1) + 1)
        return jnp.stack([one, total - one])
    lengths = jnp.asarray(split_up(number_of, total, bound, slope), jnp.int32)
    couples = (number_of - 1) // 2
    giver, taker = lengths[1:1 + 2 * couples:2], lengths[2:2 + 2 * couples:2]
    margin = jnp.minimum(giver - 1, bound - taker)
    shifted = jax.random.randint(jax.random.fold_in(rng, 1), (couples,), 0, 1 << 20) % (margin + 1)
    lengths = lengths.at[1:1 + 2 * couples:2].set(giver - shifted).at[2:2 + 2 * couples:2].set(taker + shifted)
    return lengths[jax.random.permutation(jax.random.fold_in(rng, 2), number_of)]


def gaussian(stream_key, shape, deviation, most, shards=(), kind=jnp.bfloat16):
    values = deviation * jax.random.normal(stream_key, shape, jnp.float32)
    if shards:
        values = values * block_scale(stream_key, shape, shards, -0.22, 0.18)
    return jnp.clip(values, -most, most).astype(kind)


def setup_inputs(seed: int = 0) -> dict:
    splits = jax.random.split(jax.random.key(seed), 14)
    inputs = draw_inputs(jax.random.fold_in(splits[13], 71), 0)
    norm_gain_vector = jnp.clip(1.0 + 0.1 * jax.random.normal(splits[1], (MODEL_WIDTH,), jnp.float32), 0.5, 1.5).astype(jnp.bfloat16)
    weight = gaussian(splits[2], (MODEL_WIDTH, MODEL_WIDTH), MODEL_WIDTH ** -0.5, 0.046875, ((1, 8),))
    down_adapters = gaussian(splits[3], (MODEL_WIDTH, TENANT_COUNT, ADAPTER_RANK), MODEL_WIDTH ** -0.5, 0.046875, ((0, 8),))
    up_adapters = gaussian(splits[4], (TENANT_COUNT, ADAPTER_RANK, MODEL_WIDTH), ADAPTER_RANK ** -0.5, 1.0, ((2, 8),))
    tenant = set_ends(skewed_ids(splits[5], (ROWS_ALL,), TENANT_COUNT, 2), jax.random.fold_in(splits[5], 3), 0, TENANT_COUNT - 1).astype(jnp.int32)
    tenant_slot_index = draw_tenant_slot_index(jax.random.fold_in(splits[13], 71), 0)
    live_row_count = uneven(splits[7], N_DP, (N_DP + 1) * ROWS // 2, ROWS, 0).astype(jnp.int32)
    cotangent = gaussian(splits[8], (ROWS_ALL, MODEL_WIDTH), 1.0, 6.0, ((0, 4), (1, 8)))
    down_row_factor = jnp.clip(jnp.exp(math.log(30000.0) - 4.6051702 * jax.random.uniform(splits[9], (SLOTS, MODEL_WIDTH), jnp.float32) ** block_scale(splits[9], (SLOTS, MODEL_WIDTH), ((0, 4), (1, 8)), -0.2, 0.2)), 300.0, 30000.0)
    down_column_factor = jnp.clip(jnp.exp(math.log(30000.0) - 4.6051702 * jax.random.uniform(splits[10], (SLOTS, ADAPTER_RANK), jnp.float32) ** block_scale(splits[10], (SLOTS, ADAPTER_RANK), ((0, 4),), -0.2, 0.2)), 300.0, 30000.0)
    up_row_factor = jnp.clip(jnp.exp(math.log(50.0) - 4.6051702 * jax.random.uniform(splits[11], (SLOTS, ADAPTER_RANK), jnp.float32) ** block_scale(splits[11], (SLOTS, ADAPTER_RANK), ((0, 4),), -0.2, 0.2)), 0.5, 50.0)
    up_column_factor = jnp.clip(jnp.exp(math.log(50.0) - 4.6051702 * jax.random.uniform(splits[12], (SLOTS, MODEL_WIDTH), jnp.float32) ** block_scale(splits[12], (SLOTS, MODEL_WIDTH), ((0, 4), (1, 8)), -0.2, 0.2)), 0.5, 50.0)
    return dict(inputs=inputs, norm_gain_vector=norm_gain_vector, weight=weight, down_adapters=down_adapters, up_adapters=up_adapters, tenant=tenant, tenant_slot_index=tenant_slot_index, live_row_count=live_row_count, cotangent=cotangent, down_row_factor=down_row_factor, down_column_factor=down_column_factor, up_row_factor=up_row_factor, up_column_factor=up_column_factor)


ADAPTER_SCALE = 0.5
BETA_TWO = 0.9
SQ_EPS = 1e-30
RMS_EPS = 1e-05

def reference(inputs, norm_gain_vector, weight, down_adapters, up_adapters, tenant, tenant_slot_index, live_row_count, cotangent, down_row_factor, down_column_factor, up_row_factor, up_column_factor):
    highest_precision = lax.Precision.HIGHEST
    xf = inputs.astype(jnp.float32)
    power = lax.optimization_barrier(jnp.sum(xf * xf, axis=1, keepdims=True))
    scale = lax.rsqrt(power / MODEL_WIDTH + RMS_EPS)
    normalized_input = (xf * scale * norm_gain_vector.astype(jnp.float32)).astype(jnp.bfloat16)
    pick = tenant[:, None] == jnp.arange(TENANT_COUNT, dtype=jnp.int32)[None, :]
    pick_b = pick.astype(jnp.bfloat16)
    pick_f = pick.astype(jnp.float32)
    down_flattened = down_adapters.reshape(MODEL_WIDTH, TENANT_COUNT * ADAPTER_RANK)
    up_flattened = up_adapters.reshape(TENANT_COUNT * ADAPTER_RANK, MODEL_WIDTH)
    inner_all = jnp.dot(normalized_input, down_flattened, preferred_element_type=jnp.float32)
    inner = lax.optimization_barrier(jnp.sum(inner_all.reshape(ROWS_ALL, TENANT_COUNT, ADAPTER_RANK) * pick_f[:, :, None], axis=1))
    spread_rows = (inner.astype(jnp.bfloat16)[:, None, :] * pick_b[:, :, None]).reshape(ROWS_ALL, TENANT_COUNT * ADAPTER_RANK)
    frozen_output = jnp.dot(normalized_input, weight, preferred_element_type=jnp.float32)
    adapted_output = jnp.dot(spread_rows, up_flattened, preferred_element_type=jnp.float32)
    projected = (frozen_output + ADAPTER_SCALE * adapted_output).astype(jnp.bfloat16)
    index = jnp.arange(ROWS_ALL, dtype=jnp.int32)
    live = index % ROWS < live_row_count[index // ROWS]
    output_gradient = jnp.where(live[:, None], cotangent, jnp.zeros_like(cotangent))
    back_all = jnp.dot(output_gradient, up_flattened.T, preferred_element_type=jnp.float32)
    back = lax.optimization_barrier(jnp.sum(back_all.reshape(ROWS_ALL, TENANT_COUNT, ADAPTER_RANK) * pick_f[:, :, None], axis=1))
    backward_spread_rows = (back.astype(jnp.bfloat16)[:, None, :] * pick_b[:, :, None]).reshape(ROWS_ALL, TENANT_COUNT * ADAPTER_RANK)
    frozen_input_gradient = jnp.dot(weight, output_gradient.T, preferred_element_type=jnp.float32)
    adapter_input_gradient = jnp.dot(down_flattened, backward_spread_rows.T, preferred_element_type=jnp.float32)
    normed_gradient_transposed = (frozen_input_gradient + ADAPTER_SCALE * adapter_input_gradient).astype(jnp.bfloat16)
    down_gradient = (ADAPTER_SCALE * jnp.dot(normalized_input.T, backward_spread_rows, preferred_element_type=jnp.float32)).reshape(MODEL_WIDTH, TENANT_COUNT, ADAPTER_RANK)
    up_gradient = (ADAPTER_SCALE * jnp.dot(spread_rows.T, output_gradient, preferred_element_type=jnp.float32)).reshape(TENANT_COUNT, ADAPTER_RANK, MODEL_WIDTH)
    owner_routing = (tenant_slot_index[None, :] == jnp.arange(SLOTS, dtype=jnp.int32)[:, None]).astype(jnp.float32)
    ga = jnp.einsum('st,dtr->sdr', owner_routing, down_gradient, precision=highest_precision)
    gb = jnp.einsum('st,trd->srd', owner_routing, up_gradient, precision=highest_precision)
    sq_a = ga * ga + SQ_EPS
    sq_b = gb * gb + SQ_EPS
    row_a_new = BETA_TWO * down_row_factor + (1.0 - BETA_TWO) * (lax.optimization_barrier(jnp.sum(sq_a, axis=2)) / ADAPTER_RANK)
    col_a_new = BETA_TWO * down_column_factor + (1.0 - BETA_TWO) * (lax.optimization_barrier(jnp.sum(sq_a, axis=1)) / MODEL_WIDTH)
    row_b_new = BETA_TWO * up_row_factor + (1.0 - BETA_TWO) * (lax.optimization_barrier(jnp.sum(sq_b, axis=2)) / MODEL_WIDTH)
    col_b_new = BETA_TWO * up_column_factor + (1.0 - BETA_TWO) * (lax.optimization_barrier(jnp.sum(sq_b, axis=1)) / ADAPTER_RANK)
    mean_a = lax.optimization_barrier(jnp.sum(row_a_new, axis=1)) / MODEL_WIDTH
    mean_b = lax.optimization_barrier(jnp.sum(row_b_new, axis=1)) / ADAPTER_RANK
    update_a = ga * lax.rsqrt(row_a_new[:, :, None] * col_a_new[:, None, :] / mean_a[:, None, None])
    update_b = gb * lax.rsqrt(row_b_new[:, :, None] * col_b_new[:, None, :] / mean_b[:, None, None])
    return (projected, normed_gradient_transposed, update_a, update_b, row_a_new, col_a_new, row_b_new, col_b_new)
```

```python
import functools

import jax
import jax.numpy as jnp
from jax import lax
from jax.experimental import pallas as pl
from jax.experimental.pallas import tpu as pltpu
from jax.sharding import PartitionSpec as P

ADAPTER_SCALE = 0.5
BETA_TWO = 0.9
SQ_EPS = 1e-30
RMS_EPS = 1e-05
BUFFERS = 5
LANES = 128
TILES_PER_PIECE = 80
NT = (((1,), (1,)), ((), ()))
TN = (((0,), (0,)), ((), ()))
F32, BF16 = jnp.float32, jnp.bfloat16
MESH = pl.DeviceIdType.MESH


def xor(a, b, count):
    out, bit = 0, 1
    while bit < count:
        out = out + ((a // bit + b // bit) % 2) * bit
        bit *= 2
    return out


def kernel(
    ndp, n, rank, tenants, owned, width,
    slots, live, x_hbm, gain_hbm, cot_hbm, tenant_hbm, drf_hbm, ucf_hbm, down_hbm, up_hbm, weight,
    projected, grad_t, ga, gb, row_a, col_b, stats,
    wbuf, ag, dpx, dpg, grad, acc, part, psend, prx, csend, uprx, dnrx,
    xin, cot, gain, tenant, drf, ucf, down, up,
    pk, pkm, pkh, pkrx, pkt, sm, smrx, st, strx, spread_a, spread_b, lanes, scale_col,
    wsem, in_s, ag_s, ag_sp, ag_r, dx_s, dx_r, dg_s, dg_r, sm_s, sm_r, pp_s, pp_r, ch_s, up_r, dn_r,
    pk_s, pk_r, st_s, st_r,
):
    rows, local = xin.shape
    tile = local // 2
    nq = n // 2
    count = 4 * nq
    d = lax.axis_index("dp")
    f = lax.axis_index("fsdp")
    q, c = f // 2, f % 2
    mate = 2 * q + 1 - c

    def remote(src, dst, ssem, rsem, **where):
        return pltpu.make_async_remote_copy(
            src_ref=src, dst_ref=dst, send_sem=ssem, recv_sem=rsem,
            device_id=where, device_id_type=MESH,
        )

    def order(s):
        low = q < nq // 2
        at = jnp.where(low, q, nq - 1 - q)
        t = jnp.where(s < nq - 1 - at, nq - 1 - s, s - (nq - 1 - at))
        return jnp.where(low, t, nq - 1 - t)

    def start_row(i):
        i2 = i % count
        back = i // count == 0
        s, r = i2 // 4, i2 % 4
        t = jnp.where(back, order(s), xor(q, s, nq))
        half = jnp.where(back, r // 2, r % 2)
        piece = jnp.where(back, r % 2, r // 2)
        core = jnp.where(back, (1 - c) * (1 - half) + c * half, c * (1 - half) + (1 - c) * half)
        return (2 * t + core) * local + piece * tile

    def load(i):
        return pltpu.make_async_copy(
            weight.at[pl.ds(pl.multiple_of(start_row(i), tile), tile), :],
            wbuf.at[i % BUFFERS], wsem.at[i % BUFFERS],
        )

    ins = [
        pltpu.make_async_copy(a, b, in_s.at[k])
        for k, (a, b) in enumerate(
            (
                (x_hbm, xin), (gain_hbm, gain), (cot_hbm, cot), (tenant_hbm, tenant),
                (down_hbm, down), (up_hbm, up), (drf_hbm, drf), (ucf_hbm, ucf),
            )
        )
    ]
    for k in range(4):
        ins[k].start()
    load(jnp.int32(0)).start()
    for k in range(4, 8):
        ins[k].start()
    for i in range(1, BUFFERS):
        load(jnp.int32(i)).start()

    barrier = pltpu.get_barrier_semaphore()
    for k in range(1, n):
        pl.semaphore_signal(barrier, inc=1, device_id={"fsdp": (f + k) % n}, device_id_type=MESH)
    for k in range(1, ndp):
        pl.semaphore_signal(barrier, inc=1, device_id={"dp": (d + k) % ndp}, device_id_type=MESH)

    for k in (0, 1):
        ins[k].wait()
    square = jnp.zeros((rows, LANES), F32)
    for j in range(local // LANES):
        cols = slice(j * LANES, (j + 1) * LANES)
        xf = xin[:, cols].astype(F32)
        gained = (xf * gain[j : j + 1, :].astype(F32)).astype(BF16)
        square = square + xf * xf
        dpx[d, :, cols] = gained
        piece, lo = j * LANES // tile, j * LANES % tile
        ag[f, piece, :, lo : lo + LANES] = gained
    for k in (2, 3):
        ins[k].wait()
    alive = lax.broadcasted_iota(jnp.int32, (rows, LANES), 0) < live[0]
    for j in range(local // LANES):
        cols = slice(j * LANES, (j + 1) * LANES)
        kept = jnp.where(alive, cot[:, cols].astype(F32), 0.0).astype(BF16)
        grad[:, cols] = kept
        dpg[d, :, cols] = kept

    pl.semaphore_wait(barrier, n - 1 + ndp - 1)

    def ag_up(slot, p):
        return remote(ag.at[slot, p], ag.at[slot, p], ag_s.at[slot, p, 0], ag_r.at[slot, p], fsdp=(f + 2) % n)

    def ag_down(slot, p):
        return remote(ag.at[slot, p], ag.at[slot, p], ag_s.at[slot, p, 1], ag_r.at[slot, p], fsdp=(f + n - 2) % n)

    def ag_mate(slot, p):
        return remote(ag.at[slot, p], ag.at[slot, p], ag_sp.at[slot, p], ag_r.at[slot, p], fsdp=mate)

    def ag_own(p):
        @pl.when(q + 1 < nq)
        def _():
            ag_up(f, p).start()

        @pl.when(q > 0)
        def _():
            ag_down(f, p).start()

        ag_mate(f, p).start()

    ag_own(0)

    near, far = xor(d, 1, ndp), xor(d, 2, ndp)
    relayed = ndp == 4

    def dp_x(slot, to, k):
        return remote(dpx.at[slot], dpx.at[slot], dx_s.at[k], dx_r.at[slot], dp=to)

    def dp_g(slot, to, k):
        return remote(dpg.at[slot], dpg.at[slot], dg_s.at[k], dg_r.at[slot], dp=to)

    if relayed:
        dp_x(d, near, 0).start()
        dp_g(d, far, 0).start()
        dp_g(d, near, 1).start()
        dp_x(d, far, 1).start()
    else:
        for k in range(1, ndp):
            dp_x(d, (d + k) % ndp, k - 1).start()
            dp_g(d, (d + k) % ndp, k - 1).start()

    def relay():
        dp_x(near, far, 2).wait_recv()
        dp_x(near, far, 2).start()
        dp_g(far, near, 2).wait_recv()
        dp_g(far, near, 2).start()

    place_of = lax.broadcasted_iota(jnp.int32, (tenants * rank, rows), 0) // rank
    tenant_row = tenant[...]
    picked = place_of == tenant_row
    ins[4].wait()
    ins[5].wait()
    for at, lhs, rhs in ((0, down, dpx.at[d]), (1, up, grad)):
        full = lax.dot_general(lhs[...], rhs[...], NT, preferred_element_type=F32)
        full = jnp.where(picked, full, 0.0).reshape(tenants, rank, rows)
        pk[at, 0:rank, :] = jnp.sum(full, axis=0)
    power = jnp.sum(square.T, axis=0, keepdims=True)
    pk[0, rank : rank + 8, :] = jnp.broadcast_to(power, (8, rows))
    pk[1, rank : rank + 8, :] = jnp.zeros((8, rows), F32)

    pk_mate = remote(pk.at[1 - c], pkm, pk_s.at[0], pk_r.at[0], fsdp=mate)
    pk_mate.start()

    def pk_copy(k):
        return remote(pkh, pkrx.at[k], pk_s.at[k], pk_r.at[k], fsdp=(f + 2 * k) % n)

    def pk_back():
        return remote(pkt.at[c], pkt.at[c], pk_s.at[nq], pk_r.at[nq], fsdp=mate)

    def pk_spread():
        pk_mate.wait_recv()
        pkh[...] = pk[c] + pkm[...]
        for k in range(1, nq):
            pk_copy(k).start()

    def pk_sum():
        total = pkh[...]
        for k in range(1, nq):
            pk_copy(k).wait_recv()
            total = total + pkrx[k]
        pkt[c] = total
        pk_back().start()

    def sm_copy(k):
        return remote(sm, smrx.at[d], sm_s.at[k], sm_r.at[k], dp=(d + k) % ndp)

    def pk_use():
        pk_back().wait_recv()
        scale = lax.rsqrt(pkt[0, rank : rank + 1, :] / width + RMS_EPS)
        inner = pkt[0, 0:rank, :] * scale
        back = pkt[1, 0:rank, :]
        slot = jnp.zeros((1, rows), F32)
        for t in range(tenants):
            slot = jnp.where(tenant_row == t, slots[t].astype(F32), slot)
        sm[0:rank, :] = inner.astype(BF16)
        sm[rank : 2 * rank, :] = (back * scale).astype(BF16)
        sm[2 * rank :, :] = jnp.broadcast_to(slot, (16, rows)).astype(BF16)
        for k in range(1, ndp):
            sm_copy(k).start()
        smrx[d] = sm[...]
        spread_a[...] = jnp.where(picked, jnp.tile(inner, (tenants, 1)), 0.0).astype(BF16)
        spread_b[...] = jnp.where(picked, jnp.tile(back, (tenants, 1)), 0.0).astype(BF16)
        scale_col[...] = jnp.broadcast_to(scale, (rows, rows)).T

    def chain_copy(t, p, rsem, rx, to):
        return remote(csend.at[t, p], rx.at[t, p], ch_s.at[t, p], rsem.at[t, p], fsdp=to)

    def chain_up(t, p):
        return chain_copy(t, p, up_r, uprx, (f + 2) % n)

    def chain_down(t, p):
        return chain_copy(t, p, dn_r, dnrx, (f + n - 2) % n)

    def mate_copy(t, p):
        return remote(psend.at[t, p], prx.at[t, p], pp_s.at[t, p], pp_r.at[t, p], fsdp=mate)

    def both(t, p):
        return part[t, p].astype(F32) + prx[t, p].astype(F32)

    def head(t):
        return ((t > q) & (q == 0)) | ((t < q) & (q == nq - 1))

    def chain_head(t, p):
        mate_copy(t, p).wait_recv()
        csend[t, p] = both(t, p).astype(BF16)

        @pl.when(t > q)
        def _():
            chain_up(t, p).start()

        @pl.when(t < q)
        def _():
            chain_down(t, p).start()

    def tick(j):
        k, p = (j + 1) // 2, (j + 1) % 2
        below, above = 2 * (q - k) + c, 2 * (q + k) + c

        @pl.when(q - k >= 0)
        def _():
            ag_up(below, p).wait_recv()

            @pl.when(q + 1 < nq)
            def _():
                ag_up(below, p).start()

            ag_mate(below, p).start()

        @pl.when(q + k < nq)
        def _():
            ag_down(above, p).wait_recv()

            @pl.when(q > 0)
            def _():
                ag_down(above, p).start()

            ag_mate(above, p).start()

        m = j - 1 - 2 * q

        @pl.when((q > 0) & (m >= 0) & (m < 2 * (nq - 1 - q)))
        def _():
            t, b = nq - 1 - m // 2, m % 2
            mate_copy(t, b).wait_recv()
            chain_up(t, b).wait_recv()
            csend[t, b] = (both(t, b) + uprx[t, b].astype(F32)).astype(BF16)
            chain_up(t, b).start()

        w = j - 1 - 2 * (nq - 1 - q)

        @pl.when((q < nq - 1) & (w >= 0) & (w < 2 * q))
        def _():
            t, b = w // 2, w % 2
            mate_copy(t, b).wait_recv()
            chain_down(t, b).wait_recv()
            csend[t, b] = (both(t, b) + dnrx[t, b].astype(F32)).astype(BF16)
            chain_down(t, b).start()

    period = max(TILES_PER_PIECE * rows // local, 3)
    ticks = 2 * (nq - 1)
    offset = 2
    once = [(2, pk_spread), (2, lambda: ag_own(1)), (9, pk_sum), (11, pk_use)]
    if relayed:
        once.append((13, relay))

    def events(i, lo, hi):
        for at, what in once:
            if lo <= at < hi:
                pl.when(i == at)(what)
        j1, j2 = (i - offset) // period, (i - count) // 2 - 1
        hit1 = ((i - offset) % period == 0) & (j1 >= 1) & (j1 <= ticks) & (i <= count + 2 * (j1 + 1))
        hit2 = ((i - count) % 2 == 0) & (j2 >= 1) & (j2 <= ticks) & (i < period * j2 + offset)

        @pl.when(hit1 | hit2)
        def _():
            tick(jnp.where(hit1, j1, j2))

    @pl.loop(0, count)
    def _(i):
        events(i, 0, count)
        load(i).wait()
        s, r = i // 4, i % 4
        t, p = order(s), r % 2
        out = lax.dot_general(
            wbuf[i % BUFFERS], grad[...], NT, preferred_element_type=F32
        ).astype(BF16)
        load(i + BUFFERS).start()

        @pl.when(r < 2)
        def _():
            psend[t, p] = out
            mate_copy(t, p).start()

        @pl.when(r >= 2)
        def _():
            part[t, p] = out

        @pl.when((r == 3) & head(t))
        def _():
            chain_head(t, 0)
            chain_head(t, 1)

    acc[...] = jnp.zeros_like(acc)

    @pl.loop(count, 2 * count)
    def _(i):
        events(i, count, 2 * count)
        i2 = i - count
        s, r = i2 // 4, i2 % 4
        half, p = r % 2, r // 2
        t = xor(q, s, nq)
        slot = 2 * t + c * (1 - half) + (1 - c) * half

        @pl.when(half == 1)
        def _():
            ag_mate(slot, p).wait_recv()

        load(i).wait()
        acc[...] += jnp.dot(ag[slot, p], wbuf[i % BUFFERS], preferred_element_type=F32)

        @pl.when(i + BUFFERS < 2 * count)
        def _():
            load(i + BUFFERS).start()

    if relayed:
        corner = xor(d, 3, ndp)
        for slot in (far, corner):
            dp_x(slot, far, 0).wait_recv()
        for slot in (near, corner):
            dp_g(slot, near, 0).wait_recv()
    else:
        for k in range(1, ndp):
            dp_x((d + k) % ndp, (d + 1) % ndp, 0).wait_recv()
            dp_g((d + k) % ndp, (d + 1) % ndp, 0).wait_recv()
    for k in range(1, ndp):
        sm_copy(k).wait_recv()
    ins[6].wait()
    ins[7].wait()
    place = lax.broadcasted_iota(jnp.int32, (owned * rank, rows), 0) // rank + d * owned
    place = place.astype(F32)
    for at, src, dst, summed, old, base in (
        (rank, dpx, ga, row_a, drf, 0), (0, dpg, gb, col_b, ucf, owned * rank)
    ):
        lhs = jnp.concatenate(
            [
                jnp.where(
                    place == smrx[g, 2 * rank : 2 * rank + 1, :].astype(F32),
                    jnp.tile(smrx[g, at : at + rank, :].astype(F32), (owned, 1)),
                    0.0,
                ).astype(BF16)
                for g in range(ndp)
            ],
            axis=1,
        )
        step = min(512, local)
        for lo in range(0, local, step):
            rhs = src[:, :, lo : lo + step].reshape(ndp * rows, step)
            full = ADAPTER_SCALE * jnp.dot(lhs, rhs, preferred_element_type=F32)
            full = full.reshape(owned, rank, step)
            dst[:, :, lo : lo + step] = full
            sq = full * full + SQ_EPS
            summed[:, lo : lo + step] = BETA_TWO * old[:, lo : lo + step] + (1.0 - BETA_TWO) * (
                jnp.sum(sq, axis=1) / rank
            )
            flat = sq.reshape(owned * rank, step)
            total = flat[:, 0:LANES]
            for w in range(LANES, step, LANES):
                total = total + flat[:, w : w + LANES]
            here = slice(base, base + owned * rank)
            if lo == 0:
                lanes[here, :] = total
            else:
                lanes[here, :] += total
    cols = 2 * owned * rank
    st[...] = jnp.zeros_like(st)
    factor = drf[:, 0:LANES]
    for w in range(LANES, local, LANES):
        factor = factor + drf[:, w : w + LANES]
    lanes[cols:, :] = jnp.concatenate([factor, jnp.zeros((LANES - owned, LANES), F32)], axis=0)
    for k in range(cols // LANES + 1):
        st[k : k + 1, :] = jnp.sum(lanes[k * LANES : (k + 1) * LANES, :].T, axis=0, keepdims=True)

    def st_copy(k):
        return remote(st, strx.at[k], st_s.at[k], st_r.at[k], fsdp=(f + k) % n)

    for k in range(1, n):
        st_copy(k).start()
    chunk = min(512, local)
    for lo in range(0, local, chunk):
        here = slice(lo, lo + chunk)
        adapted = lax.dot_general(spread_a[...], up[:, here], TN, preferred_element_type=F32)
        wide = jnp.concatenate([scale_col[...]] * (chunk // rows), axis=1)
        projected[:, here] = (acc[:, here] * wide + ADAPTER_SCALE * adapted).astype(BF16)

    chunk = min(512, tile)
    for p in range(2):
        mate_copy(q, p).wait_recv()

        @pl.when(q > 0)
        def _():
            chain_up(q, p).wait_recv()

        @pl.when(q < nq - 1)
        def _():
            chain_down(q, p).wait_recv()

        for lo in range(0, tile, chunk):
            here = slice(lo, lo + chunk)
            there = slice(p * tile + lo, p * tile + lo + chunk)
            out = lax.dot_general(down[:, there], spread_b[...], TN, preferred_element_type=F32)
            out = ADAPTER_SCALE * out + part[q, p, here, :].astype(F32) + prx[q, p, here, :].astype(F32)
            from_up = jnp.where(q > 0, uprx[q, p, here, :].astype(F32), 0.0)
            from_dn = jnp.where(q < nq - 1, dnrx[q, p, here, :].astype(F32), 0.0)
            grad_t[there, :] = (out + from_up + from_dn).astype(BF16)

    whole = st[...]
    for k in range(1, n):
        st_copy(k).wait_recv()
        whole = whole + strx[k]
    stats[...] = whole
    pk_mate.wait_send()
    pk_back().wait_send()
    for k in range(1, nq):
        pk_copy(k).wait_send()
    for k in range(1, n):
        st_copy(k).wait_send()
    for k in range(1, ndp):
        sm_copy(k).wait_send()
        dp_x(d, (d + 1) % ndp, k - 1).wait_send()
        dp_g(d, (d + 1) % ndp, k - 1).wait_send()

    @pl.loop(0, nq)
    def _(t):
        slot = 2 * t + c
        for p in range(2):
            mate_copy(t, p).wait_send()

            @pl.when(t != q)
            def _():
                chain_up(t, p).wait_send()

            ag_mate(slot, p).wait_send()

            @pl.when((t <= q) & (q + 1 < nq))
            def _():
                ag_up(slot, p).wait_send()

            @pl.when((t >= q) & (q > 0))
            def _():
                ag_down(slot, p).wait_send()


def finish(
    rank, owned, width,
    projected, grad_t, ga, gb, row_a, col_b, stats, dcf, urf,
    projected_out, grad_t_out, update_a_out, update_b_out, row_a_out, col_a_out, row_b_out, col_b_out,
    update_a, update_b, col_a, row_b, sems, slot_sems,
):
    copies = [
        pltpu.make_async_copy(src, dst, sems.at[k])
        for k, (src, dst) in enumerate(
            (
                (projected, projected_out), (grad_t, grad_t_out), (row_a, row_a_out), (col_b, col_b_out),
                (col_a, col_a_out), (row_b, row_b_out),
            )
        )
    ]
    for k in range(4):
        copies[k].start()
    per = LANES // rank
    lines = owned // per
    sums = [
        jnp.concatenate(
            [
                stats[base + s // per : base + s // per + 1, s % per * rank : (s % per + 1) * rank]
                for s in range(owned)
            ],
            axis=0,
        )
        for base in (0, lines)
    ]
    new_a = BETA_TWO * dcf[...] + (1.0 - BETA_TWO) * (sums[0] / width)
    new_b = BETA_TWO * urf[...] + (1.0 - BETA_TWO) * (sums[1] / width)
    col_a[...] = new_a
    row_b[...] = new_b
    for k in (4, 5):
        copies[k].start()
    line = jnp.broadcast_to(stats[2 * lines : 2 * lines + 1, :], (owned, LANES))
    own = lax.broadcasted_iota(jnp.int32, (owned, LANES), 0) == lax.broadcasted_iota(
        jnp.int32, (owned, LANES), 1
    )
    kept = jnp.sum(jnp.where(own, line, 0.0), axis=1, keepdims=True)
    mean_a = (BETA_TWO * kept + (1.0 - BETA_TWO) * (jnp.sum(sums[0], axis=1, keepdims=True) / rank)) / width
    mean_b = jnp.sum(new_b, axis=1, keepdims=True) / rank
    wide_a = lax.rsqrt(row_a[...] / mean_a)
    wide_b = lax.rsqrt(col_b[...])
    tall_a = lax.rsqrt(new_a).T
    tall_b = lax.rsqrt(new_b / mean_b).T
    work = ((ga, update_a, update_a_out, wide_a, tall_a), (gb, update_b, update_b_out, wide_b, tall_b))
    for s in range(owned):
        for which, (src, dst, out, wide, tall) in enumerate(work):
            dst[s] = src[s] * wide[s : s + 1, :] * tall[:, s : s + 1]
            copy = pltpu.make_async_copy(dst.at[s], out.at[s], slot_sems.at[which, s])
            copy.start()
            copies.append(copy)
    for copy in copies:
        copy.wait()


def on_device(
    ndp,
    n,
    inputs,
    norm_gain_vector,
    weight,
    down_adapters,
    up_adapters,
    tenant,
    tenant_slot_index,
    live_row_count,
    cotangent,
    down_row_factor,
    down_column_factor,
    up_row_factor,
    up_column_factor,
):
    rows, local = inputs.shape
    width = weight.shape[0]
    tenants, rank = down_adapters.shape[1:]
    owned = down_row_factor.shape[0]
    down = jnp.transpose(down_adapters, (1, 2, 0)).reshape(tenants * rank, local)
    up = up_adapters.reshape(tenants * rank, local)
    gain = norm_gain_vector.reshape(local // LANES, LANES)
    tile = local // 2
    nq = n // 2
    cols = 2 * owned * rank
    dma = pltpu.SemaphoreType.DMA
    piece = pltpu.VMEM((nq, 2, tile, rows), BF16)
    anywhere = pl.BlockSpec(memory_space=pl.ANY)
    vmem = pl.BlockSpec(memory_space=pltpu.VMEM)
    scalar = pl.BlockSpec(memory_space=pltpu.SMEM)
    small = pltpu.VMEM((rank + 8, rows), F32)
    results = (
        ((rows, local), BF16),
        ((local, rows), BF16),
        ((owned, rank, local), F32),
        ((owned, rank, local), F32),
        ((owned, local), F32),
        ((owned, local), F32),
        ((8, LANES), F32),
    )
    projected, grad_t, ga, gb, row_a, col_b, stats = pl.pallas_call(
        functools.partial(kernel, ndp, n, rank, tenants, owned, width),
        out_shape=tuple(pltpu.VMEM(*r) for r in results),
        in_specs=[scalar] * 2 + [anywhere] * 9,
        out_specs=(vmem,) * 7,
        scratch_shapes=[
            pltpu.VMEM((BUFFERS, tile, local), BF16),
            pltpu.VMEM((n, 2, rows, tile), BF16),
            pltpu.VMEM((ndp, rows, local), BF16),
            pltpu.VMEM((ndp, rows, local), BF16),
            pltpu.VMEM((rows, local), BF16),
            pltpu.VMEM((rows, local), F32),
            piece, piece, piece, piece, piece, piece,
            pltpu.VMEM((rows, local), BF16),
            pltpu.VMEM((rows, local), BF16),
            pltpu.VMEM((local // LANES, LANES), BF16),
            pltpu.VMEM((1, rows), jnp.int32),
            pltpu.VMEM((owned, local), F32),
            pltpu.VMEM((owned, local), F32),
            pltpu.VMEM((tenants * rank, local), BF16),
            pltpu.VMEM((tenants * rank, local), BF16),
            pltpu.VMEM((2, rank + 8, rows), F32),
            small,
            small,
            pltpu.VMEM((nq, rank + 8, rows), F32),
            pltpu.VMEM((2, rank + 8, rows), F32),
            pltpu.VMEM((2 * rank + 16, rows), BF16),
            pltpu.VMEM((ndp, 2 * rank + 16, rows), BF16),
            pltpu.VMEM((8, LANES), F32),
            pltpu.VMEM((n, 8, LANES), F32),
            pltpu.VMEM((tenants * rank, rows), BF16),
            pltpu.VMEM((tenants * rank, rows), BF16),
            pltpu.VMEM((cols + LANES, LANES), F32),
            pltpu.VMEM((rows, rows), F32),
        ]
        + [
            dma((BUFFERS,)),
            dma((8,)),
            dma((n, 2, 2)),
            dma((n, 2)),
            dma((n, 2)),
            dma((ndp,)),
            dma((ndp,)),
            dma((ndp,)),
            dma((ndp,)),
            dma((ndp,)),
            dma((ndp,)),
            dma((nq, 2)),
            dma((nq, 2)),
            dma((nq, 2)),
            dma((nq, 2)),
            dma((nq, 2)),
            dma((nq + 1,)),
            dma((nq + 1,)),
            dma((n,)),
            dma((n,)),
        ],
        compiler_params=pltpu.CompilerParams(
            collective_id=0, has_side_effects=True, vmem_limit_bytes=54 * 1024 * 1024
        ),
    )(
        tenant_slot_index, live_row_count, inputs, gain, cotangent, tenant.reshape(1, rows),
        down_row_factor, up_column_factor, down, up, weight,
    )

    shapes = (
        ((rows, local), BF16),
        ((local, rows), BF16),
        ((owned, rank, local), F32),
        ((owned, rank, local), F32),
        ((owned, local), F32),
        ((owned, rank), F32),
        ((owned, rank), F32),
        ((owned, local), F32),
    )
    outs = pl.pallas_call(
        functools.partial(finish, rank, owned, width),
        out_shape=tuple(jax.ShapeDtypeStruct(*r) for r in shapes),
        in_specs=[vmem] * 9,
        out_specs=(anywhere,) * 8,
        scratch_shapes=[
            pltpu.VMEM((owned, rank, local), F32),
            pltpu.VMEM((owned, rank, local), F32),
            pltpu.VMEM((owned, rank), F32),
            pltpu.VMEM((owned, rank), F32),
            dma((6,)),
            dma((2, owned)),
        ],
        compiler_params=pltpu.CompilerParams(vmem_limit_bytes=16 * 1024 * 1024),
    )(projected, grad_t, ga, gb, row_a, col_b, stats, down_column_factor, up_row_factor)
    return outs[:2] + (jnp.swapaxes(outs[2], 1, 2),) + outs[3:]


def solution(mesh):
    return jax.shard_map(
        functools.partial(on_device, mesh.shape["dp"], mesh.shape["fsdp"]),
        mesh=mesh,
        in_specs=(
            P("dp", "fsdp"),
            P("fsdp"),
            P(None, "fsdp"),
            P("fsdp", None, None),
            P(None, None, "fsdp"),
            P("dp"),
            P(),
            P("dp"),
            P("dp", "fsdp"),
            P("dp", "fsdp"),
            P("dp", None),
            P("dp", None),
            P("dp", "fsdp"),
        ),
        out_specs=(
            P("dp", "fsdp"),
            P("fsdp", "dp"),
            P("dp", "fsdp", None),
            P("dp", None, "fsdp"),
            P("dp", "fsdp"),
            P("dp", None),
            P("dp", None),
            P("dp", "fsdp"),
        ),
        check_vma=False,
    )
```

```python
import functools

import jax
import jax.numpy as jnp
from jax import lax
from jax.experimental import pallas as pl
from jax.experimental.pallas import tpu as pltpu
from jax.sharding import PartitionSpec as P

ADAPTER_SCALE = 0.5
BETA_TWO = 0.9
SQ_EPS = 1e-30
RMS_EPS = 1e-05
BUFFERS = 5
LANES = 128
TILES_PER_PIECE = 80
NT = (((1,), (1,)), ((), ()))
TN = (((0,), (0,)), ((), ()))
F32, BF16 = jnp.float32, jnp.bfloat16
MESH = pl.DeviceIdType.MESH


def xor(a, b, count):
    out, bit = 0, 1
    while bit < count:
        out = out + ((a // bit + b // bit) % 2) * bit
        bit *= 2
    return out


def kernel(
    ndp, n, rank, tenants, owned, width,
    slots, live, x_hbm, gain_hbm, cot_hbm, tenant_hbm, drf_hbm, ucf_hbm, down_hbm, up_hbm, weight,
    projected, grad_t, ga, gb, row_a, col_b, stats,
    wbuf, ag, dpx, dpg, grad, acc, part, psend, prx, csend, uprx, dnrx,
    xin, cot, gain, tenant, drf, ucf, down, up,
    pk, pkm, pkh, pksu, pksd, pku, pkd, pkt, sm, smrx, st, strx, spread_a, spread_b, lanes, scale_col, base,
    wsem, in_s, ag_s, ag_sp, ag_r, dx_s, dx_r, dg_s, dg_r, sm_s, sm_r, pp_s, pp_r, ch_s, up_r, dn_r,
    pk_s, pk_r, st_s, st_r,
):
    rows, local = xin.shape
    tile = local // 2
    nq = n // 2
    count = 4 * nq
    d = lax.axis_index("dp")
    f = lax.axis_index("fsdp")
    q, c = f // 2, f % 2
    mate = 2 * q + 1 - c

    def remote(src, dst, ssem, rsem, **where):
        return pltpu.make_async_remote_copy(
            src_ref=src, dst_ref=dst, send_sem=ssem, recv_sem=rsem,
            device_id=where, device_id_type=MESH,
        )

    def order(s):
        low = q < nq // 2
        at = jnp.where(low, q, nq - 1 - q)
        t = jnp.where(s < nq - 1 - at, nq - 1 - s, s - (nq - 1 - at))
        return jnp.where(low, t, nq - 1 - t)

    def start_row(i):
        i2 = i % count
        back = i // count == 0
        s, r = i2 // 4, i2 % 4
        t = jnp.where(back, order(s), xor(q, s, nq))
        half = jnp.where(back, r // 2, r % 2)
        piece = jnp.where(back, r % 2, r // 2)
        core = jnp.where(back, (1 - c) * (1 - half) + c * half, c * (1 - half) + (1 - c) * half)
        return (2 * t + core) * local + piece * tile

    def load(i):
        return pltpu.make_async_copy(
            weight.at[pl.ds(pl.multiple_of(start_row(i), tile), tile), :],
            wbuf.at[i % BUFFERS], wsem.at[i % BUFFERS],
        )

    ins = [
        pltpu.make_async_copy(a, b, in_s.at[k])
        for k, (a, b) in enumerate(
            (
                (gain_hbm, gain), (x_hbm.at[:, 0:tile], xin.at[:, 0:tile]),
                (x_hbm.at[:, tile:local], xin.at[:, tile:local]), (cot_hbm, cot), (tenant_hbm, tenant),
                (down_hbm, down), (up_hbm, up), (drf_hbm, drf), (ucf_hbm, ucf),
            )
        )
    ]
    for k in range(5):
        ins[k].start()
    load(jnp.int32(0)).start()
    for k in range(5, 9):
        ins[k].start()
    for i in range(1, BUFFERS):
        load(jnp.int32(i)).start()

    barrier = pltpu.get_barrier_semaphore()

    def greet(**where):
        pl.semaphore_signal(barrier, inc=1, device_id=where, device_id_type=MESH)

    for k in range(1, ndp):
        greet(dp=(d + k) % ndp)
    greet(fsdp=mate)

    @pl.when(q + 1 < nq)
    def _():
        greet(fsdp=(f + 2) % n)

    @pl.when(q > 0)
    def _():
        greet(fsdp=(f + n - 2) % n)

    def ag_up(slot, p):
        return remote(ag.at[slot, p], ag.at[slot, p], ag_s.at[slot, p, 0], ag_r.at[slot, p], fsdp=(f + 2) % n)

    def ag_down(slot, p):
        return remote(ag.at[slot, p], ag.at[slot, p], ag_s.at[slot, p, 1], ag_r.at[slot, p], fsdp=(f + n - 2) % n)

    def ag_mate(slot, p):
        return remote(ag.at[slot, p], ag.at[slot, p], ag_sp.at[slot, p], ag_r.at[slot, p], fsdp=mate)

    def ag_own(p):
        @pl.when(q + 1 < nq)
        def _():
            ag_up(f, p).start()

        @pl.when(q > 0)
        def _():
            ag_down(f, p).start()

        ag_mate(f, p).start()

    def prepare(p, square):
        for j in range(p * tile // LANES, (p + 1) * tile // LANES):
            cols = slice(j * LANES, (j + 1) * LANES)
            xf = xin[:, cols].astype(F32)
            gained = (xf * gain[j : j + 1, :].astype(F32)).astype(BF16)
            square = square + xf * xf
            dpx[d, :, cols] = gained
            ag[f, p, :, j * LANES - p * tile : (j + 1) * LANES - p * tile] = gained
        return square

    ins[0].wait()
    ins[1].wait()
    square = prepare(0, jnp.zeros((rows, LANES), F32))
    pl.semaphore_wait(barrier, ndp + (q + 1 < nq).astype(jnp.int32) + (q > 0).astype(jnp.int32))
    ag_own(0)
    ins[2].wait()
    square = prepare(1, square)

    near, far = xor(d, 1, ndp), xor(d, 2, ndp)
    relayed = ndp == 4

    def dp_x(slot, to, k):
        return remote(dpx.at[slot], dpx.at[slot], dx_s.at[k], dx_r.at[slot], dp=to)

    def dp_g(slot, to, k):
        return remote(dpg.at[slot], dpg.at[slot], dg_s.at[k], dg_r.at[slot], dp=to)

    if relayed:
        dp_x(d, near, 0).start()
    ins[3].wait()
    ins[4].wait()
    alive = lax.broadcasted_iota(jnp.int32, (rows, LANES), 0) < live[0]
    for j in range(local // LANES):
        cols = slice(j * LANES, (j + 1) * LANES)
        kept = jnp.where(alive, cot[:, cols].astype(F32), 0.0).astype(BF16)
        grad[:, cols] = kept
        dpg[d, :, cols] = kept
    if relayed:
        dp_g(d, far, 0).start()
        dp_g(d, near, 1).start()
        dp_x(d, far, 1).start()
    else:
        for k in range(1, ndp):
            dp_x(d, (d + k) % ndp, k - 1).start()
            dp_g(d, (d + k) % ndp, k - 1).start()

    def relay():
        dp_x(near, far, 2).wait_recv()
        dp_x(near, far, 2).start()
        dp_g(far, near, 2).wait_recv()
        dp_g(far, near, 2).start()

    place_of = lax.broadcasted_iota(jnp.int32, (tenants * rank, rows), 0) // rank
    tenant_row = tenant[...]
    picked = place_of == tenant_row
    ins[5].wait()
    ins[6].wait()
    for at, lhs, rhs in ((0, down, dpx.at[d]), (1, up, grad)):
        full = lax.dot_general(lhs[...], rhs[...], NT, preferred_element_type=F32)
        full = jnp.where(picked, full, 0.0).reshape(tenants, rank, rows)
        pk[at, 0:rank, :] = jnp.sum(full, axis=0)
    power = jnp.sum(square.T, axis=0, keepdims=True)
    pk[0, rank : rank + 8, :] = jnp.broadcast_to(power, (8, rows))
    pk[1, rank : rank + 8, :] = jnp.zeros((8, rows), F32)

    pk_mate = remote(pk.at[1 - c], pkm, pk_s.at[0], pk_r.at[0], fsdp=mate)
    pk_mate.start()

    def pk_up():
        return remote(pksu, pku, pk_s.at[1], pk_r.at[1], fsdp=(f + 2) % n)

    def pk_down():
        return remote(pksd, pkd, pk_s.at[2], pk_r.at[2], fsdp=(f + n - 2) % n)

    def pk_back():
        return remote(pkt.at[c], pkt.at[c], pk_s.at[3], pk_r.at[3], fsdp=mate)

    def pk_spread():
        pk_mate.wait_recv()
        pkh[...] = pk[c] + pkm[...]

        @pl.when(q == 0)
        def _():
            pksu[...] = pkh[...]
            pk_up().start()

        @pl.when(q == nq - 1)
        def _():
            pksd[...] = pkh[...]
            pk_down().start()

    def pk_hop(j):
        @pl.when(q == j)
        def _():
            pk_up().wait_recv()

            @pl.when(q + 1 < nq)
            def _():
                pksu[...] = pkh[...] + pku[...]
                pk_up().start()

        @pl.when(nq - 1 - q == j)
        def _():
            pk_down().wait_recv()

            @pl.when(q > 0)
            def _():
                pksd[...] = pkh[...] + pkd[...]
                pk_down().start()

    def pk_sum():
        below = jnp.where(q > 0, pku[...], 0.0)
        above = jnp.where(q + 1 < nq, pkd[...], 0.0)
        pkt[c] = pkh[...] + below + above
        pk_back().start()

    def sm_copy(k):
        return remote(sm, smrx.at[d], sm_s.at[k], sm_r.at[k], dp=(d + k) % ndp)

    def pk_use():
        pk_back().wait_recv()
        scale = lax.rsqrt(pkt[0, rank : rank + 1, :] / width + RMS_EPS)
        inner = pkt[0, 0:rank, :] * scale
        back = pkt[1, 0:rank, :]
        slot = jnp.zeros((1, rows), F32)
        for t in range(tenants):
            slot = jnp.where(tenant_row == t, slots[t].astype(F32), slot)
        sm[0:rank, :] = inner.astype(BF16)
        sm[rank : 2 * rank, :] = (back * scale).astype(BF16)
        sm[2 * rank :, :] = jnp.broadcast_to(slot, (16, rows)).astype(BF16)
        for k in range(1, ndp):
            sm_copy(k).start()
        smrx[d] = sm[...]
        spread_a[...] = jnp.where(picked, jnp.tile(inner, (tenants, 1)), 0.0).astype(BF16)
        spread_b[...] = jnp.where(picked, jnp.tile(back, (tenants, 1)), 0.0).astype(BF16)
        scale_col[...] = jnp.broadcast_to(scale, (rows, rows)).T

    def chain_copy(t, p, h, rsem, rx, to):
        part_of = pl.ds(h * (tile // 2), tile // 2)
        return remote(
            csend.at[t, p, part_of], rx.at[t, p, part_of], ch_s.at[t, p, h], rsem.at[t, p, h], fsdp=to
        )

    def chain_up(t, p, h):
        return chain_copy(t, p, h, up_r, uprx, (f + 2) % n)

    def chain_down(t, p, h):
        return chain_copy(t, p, h, dn_r, dnrx, (f + n - 2) % n)

    def send_up(t, p):
        chain_up(t, p, 0).start()

        @pl.when((t != q + 1) | (p == 0))
        def _():
            chain_up(t, p, 1).start()

    def send_down(t, p):
        chain_down(t, p, 0).start()

        @pl.when((t != q - 1) | (p == 0))
        def _():
            chain_down(t, p, 1).start()

    def mate_copy(t, p):
        return remote(psend.at[t, p], prx.at[t, p], pp_s.at[t, p], pp_r.at[t, p], fsdp=mate)

    def both(t, p):
        return part[t, p].astype(F32) + prx[t, p].astype(F32)

    def head(t):
        return ((t > q) & (q == 0)) | ((t < q) & (q == nq - 1))

    def chain_head(t, p):
        mate_copy(t, p).wait_recv()
        csend[t, p] = both(t, p).astype(BF16)

        @pl.when(t > q)
        def _():
            send_up(t, p)

        @pl.when(t < q)
        def _():
            send_down(t, p)

    def tick(j):
        k, p = (j + 1) // 2, (j + 1) % 2
        below, above = 2 * (q - k) + c, 2 * (q + k) + c

        @pl.when(q - k >= 0)
        def _():
            ag_up(below, p).wait_recv()

            @pl.when(q + 1 < nq)
            def _():
                ag_up(below, p).start()

            ag_mate(below, p).start()

        @pl.when(q + k < nq)
        def _():
            ag_down(above, p).wait_recv()

            @pl.when(q > 0)
            def _():
                ag_down(above, p).start()

            ag_mate(above, p).start()

        pk_hop(j)
        m = j - 1 - 2 * q

        @pl.when((q > 0) & (m >= 0) & (m < 2 * (nq - 1 - q)))
        def _():
            t, b = nq - 1 - m // 2, m % 2
            mate_copy(t, b).wait_recv()
            for h in range(2):
                chain_up(t, b, h).wait_recv()
            csend[t, b] = (both(t, b) + uprx[t, b].astype(F32)).astype(BF16)
            send_up(t, b)

        w = j - 1 - 2 * (nq - 1 - q)

        @pl.when((q < nq - 1) & (w >= 0) & (w < 2 * q))
        def _():
            t, b = w // 2, w % 2
            mate_copy(t, b).wait_recv()
            for h in range(2):
                chain_down(t, b, h).wait_recv()
            csend[t, b] = (both(t, b) + dnrx[t, b].astype(F32)).astype(BF16)
            send_down(t, b)

    period = max(TILES_PER_PIECE * rows // local, 3)
    ticks = 2 * (nq - 1)
    offset = -1
    chained = min(period * (nq - 1) + offset, count + 2 * nq)
    once = [(2, pk_spread), (2, lambda: ag_own(1)), (chained + 1, pk_sum), (chained + 3, pk_use)]
    if relayed:
        once.append((13, relay))

    def events(i, lo, hi):
        for at, what in once:
            if lo <= at < hi:
                pl.when(i == at)(what)
        j1, j2 = (i - offset) // period, (i - count) // 2 - 1
        hit1 = ((i - offset) % period == 0) & (j1 >= 1) & (j1 <= ticks) & (i <= count + 2 * (j1 + 1))
        hit2 = ((i - count) % 2 == 0) & (j2 >= 1) & (j2 <= ticks) & (i < period * j2 + offset)

        @pl.when(hit1 | hit2)
        def _():
            tick(jnp.where(hit1, j1, j2))

    @pl.loop(0, count)
    def _(i):
        events(i, 0, count)
        load(i).wait()
        s, r = i // 4, i % 4
        t, p = order(s), r % 2
        out = lax.dot_general(
            wbuf[i % BUFFERS], grad[...], NT, preferred_element_type=F32
        ).astype(BF16)
        load(i + BUFFERS).start()

        @pl.when(r < 2)
        def _():
            psend[t, p] = out
            mate_copy(t, p).start()

        @pl.when(r >= 2)
        def _():
            part[t, p] = out

        @pl.when((r == 3) & head(t))
        def _():
            chain_head(t, 0)
            chain_head(t, 1)

    acc[...] = jnp.zeros_like(acc)

    @pl.loop(count, 2 * count)
    def _(i):
        events(i, count, 2 * count)
        i2 = i - count
        s, r = i2 // 4, i2 % 4
        half, p = r % 2, r // 2
        t = xor(q, s, nq)
        slot = 2 * t + c * (1 - half) + (1 - c) * half

        @pl.when(half == 1)
        def _():
            ag_mate(slot, p).wait_recv()

        load(i).wait()
        acc[...] += jnp.dot(ag[slot, p], wbuf[i % BUFFERS], preferred_element_type=F32)

        @pl.when(i + BUFFERS < 2 * count)
        def _():
            load(i + BUFFERS).start()

    if relayed:
        corner = xor(d, 3, ndp)
        for slot in (far, corner):
            dp_x(slot, far, 0).wait_recv()
        for slot in (near, corner):
            dp_g(slot, near, 0).wait_recv()
    else:
        for k in range(1, ndp):
            dp_x((d + k) % ndp, (d + 1) % ndp, 0).wait_recv()
            dp_g((d + k) % ndp, (d + 1) % ndp, 0).wait_recv()
    for k in range(1, ndp):
        sm_copy(k).wait_recv()
    ins[7].wait()
    ins[8].wait()
    place = lax.broadcasted_iota(jnp.int32, (owned * rank, rows), 0) // rank + d * owned
    place = place.astype(F32)
    for at, src, dst, summed, old, line in (
        (rank, dpx, ga, row_a, drf, 0), (0, dpg, gb, col_b, ucf, owned * rank)
    ):
        lhs = jnp.concatenate(
            [
                jnp.where(
                    place == smrx[g, 2 * rank : 2 * rank + 1, :].astype(F32),
                    jnp.tile(smrx[g, at : at + rank, :].astype(F32), (owned, 1)),
                    0.0,
                ).astype(BF16)
                for g in range(ndp)
            ],
            axis=1,
        )
        step = min(512, local)
        for lo in range(0, local, step):
            rhs = src[:, :, lo : lo + step].reshape(ndp * rows, step)
            full = ADAPTER_SCALE * jnp.dot(lhs, rhs, preferred_element_type=F32)
            full = full.reshape(owned, rank, step)
            dst[:, :, lo : lo + step] = full
            sq = full * full + SQ_EPS
            summed[:, lo : lo + step] = BETA_TWO * old[:, lo : lo + step] + (1.0 - BETA_TWO) * (
                jnp.sum(sq, axis=1) / rank
            )
            flat = sq.reshape(owned * rank, step)
            total = flat[:, 0:LANES]
            for w in range(LANES, step, LANES):
                total = total + flat[:, w : w + LANES]
            here = slice(line, line + owned * rank)
            if lo == 0:
                lanes[here, :] = total
            else:
                lanes[here, :] += total
    cols = 2 * owned * rank
    st[...] = jnp.zeros_like(st)
    factor = drf[:, 0:LANES]
    for w in range(LANES, local, LANES):
        factor = factor + drf[:, w : w + LANES]
    lanes[cols:, :] = jnp.concatenate([factor, jnp.zeros((LANES - owned, LANES), F32)], axis=0)
    for k in range(cols // LANES + 1):
        st[k : k + 1, :] = jnp.sum(lanes[k * LANES : (k + 1) * LANES, :].T, axis=0, keepdims=True)

    def st_copy(k):
        return remote(st, strx.at[k], st_s.at[k], st_r.at[k], fsdp=(f + k) % n)

    for k in range(1, n):
        st_copy(k).start()

    @pl.when(q + 1 < nq)
    def _():
        chain_up(q + 1, 1, 1).start()

    @pl.when(q > 0)
    def _():
        chain_down(q - 1, 1, 1).start()
    chunk = min(512, local)
    for lo in range(0, local, chunk):
        here = slice(lo, lo + chunk)
        adapted = lax.dot_general(spread_a[...], up[:, here], TN, preferred_element_type=F32)
        wide = jnp.concatenate([scale_col[...]] * (chunk // rows), axis=1)
        projected[:, here] = (acc[:, here] * wide + ADAPTER_SCALE * adapted).astype(BF16)

    quarter = tile // 2
    for p in range(2):
        mate_copy(q, p).wait_recv()
        for h in range(2):
            here = slice(h * quarter, (h + 1) * quarter)
            there = slice(p * tile + h * quarter, p * tile + (h + 1) * quarter)
            out = lax.dot_general(down[:, there], spread_b[...], TN, preferred_element_type=F32)
            out = ADAPTER_SCALE * out + part[q, p, here, :].astype(F32) + prx[q, p, here, :].astype(F32)
            base[there, :] = out
    for p in range(2):
        for h in range(2):
            here = slice(h * quarter, (h + 1) * quarter)
            there = slice(p * tile + h * quarter, p * tile + (h + 1) * quarter)

            @pl.when(q > 0)
            def _():
                chain_up(q, p, h).wait_recv()

            @pl.when(q < nq - 1)
            def _():
                chain_down(q, p, h).wait_recv()

            from_up = jnp.where(q > 0, uprx[q, p, here, :].astype(F32), 0.0)
            from_dn = jnp.where(q < nq - 1, dnrx[q, p, here, :].astype(F32), 0.0)
            grad_t[there, :] = (base[there, :] + from_up + from_dn).astype(BF16)

    whole = st[...]
    for k in range(1, n):
        st_copy(k).wait_recv()
        whole = whole + strx[k]
    stats[...] = whole
    pk_mate.wait_send()
    pk_back().wait_send()

    @pl.when(q + 1 < nq)
    def _():
        pk_up().wait_send()

    @pl.when(q > 0)
    def _():
        pk_down().wait_send()

    for k in range(1, n):
        st_copy(k).wait_send()
    for k in range(1, ndp):
        sm_copy(k).wait_send()
        dp_x(d, (d + 1) % ndp, k - 1).wait_send()
        dp_g(d, (d + 1) % ndp, k - 1).wait_send()

    @pl.loop(0, nq)
    def _(t):
        slot = 2 * t + c
        for p in range(2):
            mate_copy(t, p).wait_send()

            @pl.when(t != q)
            def _():
                for h in range(2):
                    chain_up(t, p, h).wait_send()

            ag_mate(slot, p).wait_send()

            @pl.when((t <= q) & (q + 1 < nq))
            def _():
                ag_up(slot, p).wait_send()

            @pl.when((t >= q) & (q > 0))
            def _():
                ag_down(slot, p).wait_send()


def finish(
    rank, owned, width,
    projected, grad_t, ga, gb, row_a, col_b, stats, dcf, urf,
    projected_out, grad_t_out, update_a_out, update_b_out, row_a_out, col_a_out, row_b_out, col_b_out,
    update_a, update_b, col_a, row_b, sems, slot_sems,
):
    copies = [
        pltpu.make_async_copy(src, dst, sems.at[k])
        for k, (src, dst) in enumerate(
            (
                (projected, projected_out), (grad_t, grad_t_out), (row_a, row_a_out), (col_b, col_b_out),
                (col_a, col_a_out), (row_b, row_b_out),
            )
        )
    ]
    for k in range(4):
        copies[k].start()
    per = LANES // rank
    lines = owned // per
    sums = [
        jnp.concatenate(
            [
                stats[base + s // per : base + s // per + 1, s % per * rank : (s % per + 1) * rank]
                for s in range(owned)
            ],
            axis=0,
        )
        for base in (0, lines)
    ]
    new_a = BETA_TWO * dcf[...] + (1.0 - BETA_TWO) * (sums[0] / width)
    new_b = BETA_TWO * urf[...] + (1.0 - BETA_TWO) * (sums[1] / width)
    col_a[...] = new_a
    row_b[...] = new_b
    for k in (4, 5):
        copies[k].start()
    line = jnp.broadcast_to(stats[2 * lines : 2 * lines + 1, :], (owned, LANES))
    own = lax.broadcasted_iota(jnp.int32, (owned, LANES), 0) == lax.broadcasted_iota(
        jnp.int32, (owned, LANES), 1
    )
    kept = jnp.sum(jnp.where(own, line, 0.0), axis=1, keepdims=True)
    mean_a = (BETA_TWO * kept + (1.0 - BETA_TWO) * (jnp.sum(sums[0], axis=1, keepdims=True) / rank)) / width
    mean_b = jnp.sum(new_b, axis=1, keepdims=True) / rank
    wide_a = lax.rsqrt(row_a[...] / mean_a)
    wide_b = lax.rsqrt(col_b[...])
    tall_a = lax.rsqrt(new_a).T
    tall_b = lax.rsqrt(new_b / mean_b).T
    work = ((ga, update_a, update_a_out, wide_a, tall_a), (gb, update_b, update_b_out, wide_b, tall_b))
    for s in range(owned):
        for which, (src, dst, out, wide, tall) in enumerate(work):
            dst[s] = src[s] * wide[s : s + 1, :] * tall[:, s : s + 1]
            copy = pltpu.make_async_copy(dst.at[s], out.at[s], slot_sems.at[which, s])
            copy.start()
            copies.append(copy)
    for copy in copies:
        copy.wait()


def on_device(
    ndp,
    n,
    inputs,
    norm_gain_vector,
    weight,
    down_adapters,
    up_adapters,
    tenant,
    tenant_slot_index,
    live_row_count,
    cotangent,
    down_row_factor,
    down_column_factor,
    up_row_factor,
    up_column_factor,
):
    rows, local = inputs.shape
    width = weight.shape[0]
    tenants, rank = down_adapters.shape[1:]
    owned = down_row_factor.shape[0]
    down = jnp.transpose(down_adapters, (1, 2, 0)).reshape(tenants * rank, local)
    up = up_adapters.reshape(tenants * rank, local)
    gain = norm_gain_vector.reshape(local // LANES, LANES)
    tile = local // 2
    nq = n // 2
    cols = 2 * owned * rank
    dma = pltpu.SemaphoreType.DMA
    piece = pltpu.VMEM((nq, 2, tile, rows), BF16)
    anywhere = pl.BlockSpec(memory_space=pl.ANY)
    vmem = pl.BlockSpec(memory_space=pltpu.VMEM)
    scalar = pl.BlockSpec(memory_space=pltpu.SMEM)
    small = pltpu.VMEM((rank + 8, rows), F32)
    results = (
        ((rows, local), BF16),
        ((local, rows), BF16),
        ((owned, rank, local), F32),
        ((owned, rank, local), F32),
        ((owned, local), F32),
        ((owned, local), F32),
        ((8, LANES), F32),
    )
    projected, grad_t, ga, gb, row_a, col_b, stats = pl.pallas_call(
        functools.partial(kernel, ndp, n, rank, tenants, owned, width),
        out_shape=tuple(pltpu.VMEM(*r) for r in results),
        in_specs=[scalar] * 2 + [anywhere] * 9,
        out_specs=(vmem,) * 7,
        scratch_shapes=[
            pltpu.VMEM((BUFFERS, tile, local), BF16),
            pltpu.VMEM((n, 2, rows, tile), BF16),
            pltpu.VMEM((ndp, rows, local), BF16),
            pltpu.VMEM((ndp, rows, local), BF16),
            pltpu.VMEM((rows, local), BF16),
            pltpu.VMEM((rows, local), F32),
            piece, piece, piece, piece, piece, piece,
            pltpu.VMEM((rows, local), BF16),
            pltpu.VMEM((rows, local), BF16),
            pltpu.VMEM((local // LANES, LANES), BF16),
            pltpu.VMEM((1, rows), jnp.int32),
            pltpu.VMEM((owned, local), F32),
            pltpu.VMEM((owned, local), F32),
            pltpu.VMEM((tenants * rank, local), BF16),
            pltpu.VMEM((tenants * rank, local), BF16),
            pltpu.VMEM((2, rank + 8, rows), F32),
            small, small, small, small, small, small,
            pltpu.VMEM((2, rank + 8, rows), F32),
            pltpu.VMEM((2 * rank + 16, rows), BF16),
            pltpu.VMEM((ndp, 2 * rank + 16, rows), BF16),
            pltpu.VMEM((8, LANES), F32),
            pltpu.VMEM((n, 8, LANES), F32),
            pltpu.VMEM((tenants * rank, rows), BF16),
            pltpu.VMEM((tenants * rank, rows), BF16),
            pltpu.VMEM((cols + LANES, LANES), F32),
            pltpu.VMEM((rows, rows), F32),
            pltpu.VMEM((local, rows), F32),
        ]
        + [
            dma((BUFFERS,)),
            dma((9,)),
            dma((n, 2, 2)),
            dma((n, 2)),
            dma((n, 2)),
            dma((ndp,)),
            dma((ndp,)),
            dma((ndp,)),
            dma((ndp,)),
            dma((ndp,)),
            dma((ndp,)),
            dma((nq, 2)),
            dma((nq, 2)),
            dma((nq, 2, 2)),
            dma((nq, 2, 2)),
            dma((nq, 2, 2)),
            dma((4,)),
            dma((4,)),
            dma((n,)),
            dma((n,)),
        ],
        compiler_params=pltpu.CompilerParams(
            collective_id=0, has_side_effects=True, vmem_limit_bytes=54 * 1024 * 1024
        ),
    )(
        tenant_slot_index, live_row_count, inputs, gain, cotangent, tenant.reshape(1, rows),
        down_row_factor, up_column_factor, down, up, weight,
    )

    shapes = (
        ((rows, local), BF16),
        ((local, rows), BF16),
        ((owned, rank, local), F32),
        ((owned, rank, local), F32),
        ((owned, local), F32),
        ((owned, rank), F32),
        ((owned, rank), F32),
        ((owned, local), F32),
    )
    outs = pl.pallas_call(
        functools.partial(finish, rank, owned, width),
        out_shape=tuple(jax.ShapeDtypeStruct(*r) for r in shapes),
        in_specs=[vmem] * 9,
        out_specs=(anywhere,) * 8,
        scratch_shapes=[
            pltpu.VMEM((owned, rank, local), F32),
            pltpu.VMEM((owned, rank, local), F32),
            pltpu.VMEM((owned, rank), F32),
            pltpu.VMEM((owned, rank), F32),
            dma((6,)),
            dma((2, owned)),
        ],
        compiler_params=pltpu.CompilerParams(vmem_limit_bytes=16 * 1024 * 1024),
    )(projected, grad_t, ga, gb, row_a, col_b, stats, down_column_factor, up_row_factor)
    return outs[:2] + (jnp.swapaxes(outs[2], 1, 2),) + outs[3:]


def solution(mesh):
    return jax.shard_map(
        functools.partial(on_device, mesh.shape["dp"], mesh.shape["fsdp"]),
        mesh=mesh,
        in_specs=(
            P("dp", "fsdp"),
            P("fsdp"),
            P(None, "fsdp"),
            P("fsdp", None, None),
            P(None, None, "fsdp"),
            P("dp"),
            P(),
            P("dp"),
            P("dp", "fsdp"),
            P("dp", "fsdp"),
            P("dp", None),
            P("dp", None),
            P("dp", "fsdp"),
        ),
        out_specs=(
            P("dp", "fsdp"),
            P("fsdp", "dp"),
            P("dp", "fsdp", None),
            P("dp", None, "fsdp"),
            P("dp", "fsdp"),
            P("dp", None),
            P("dp", None),
            P("dp", "fsdp"),
        ),
        check_vma=False,
    )
```

```python
import functools

import jax
import jax.numpy as jnp
from jax import lax
from jax.experimental import pallas as pl
from jax.experimental.pallas import tpu as pltpu
from jax.sharding import PartitionSpec as P

ADAPTER_SCALE = 0.5
BETA_TWO = 0.9
SQ_EPS = 1e-30
RMS_EPS = 1e-05
BUFFERS = 5
LANES = 128
TILES_PER_PIECE = 80
NT = (((1,), (1,)), ((), ()))
TN = (((0,), (0,)), ((), ()))
F32, BF16 = jnp.float32, jnp.bfloat16
MESH = pl.DeviceIdType.MESH


def xor(a, b, count):
    out, bit = 0, 1
    while bit < count:
        out = out + ((a // bit + b // bit) % 2) * bit
        bit *= 2
    return out


def kernel(
    ndp, n, rank, tenants, owned, width,
    slots, live, x_hbm, gain_hbm, cot_hbm, tenant_hbm, drf_hbm, ucf_hbm, down_hbm, up_hbm, weight,
    projected, grad_t, ga, gb, row_a, col_b, stats,
    wbuf, ag, dpx, dpg, grad, acc, part, psend, prx, csend, uprx, dnrx,
    xin, cot, gain, tenant, drf, ucf, down, up,
    pk, pkm, pkh, pksu, pksd, pku, pkd, pkt, sm, smrx, st, strx, spread_a, spread_b, lanes, scale_col, base,
    wsem, in_s, ag_s, ag_sp, ag_r, dx_s, dx_r, dg_s, dg_r, sm_s, sm_r, pp_s, pp_r, ch_s, up_r, dn_r,
    pk_s, pk_r, st_s, st_r,
):
    rows, local = xin.shape
    tile = local // 2
    nq = n // 2
    count = 4 * nq
    d = lax.axis_index("dp")
    f = lax.axis_index("fsdp")
    q, c = f // 2, f % 2
    mate = 2 * q + 1 - c

    def remote(src, dst, ssem, rsem, **where):
        return pltpu.make_async_remote_copy(
            src_ref=src, dst_ref=dst, send_sem=ssem, recv_sem=rsem,
            device_id=where, device_id_type=MESH,
        )

    def order(s):
        low = q < nq // 2
        at = jnp.where(low, q, nq - 1 - q)
        t = jnp.where(s < nq - 1 - at, nq - 1 - s, s - (nq - 1 - at))
        return jnp.where(low, t, nq - 1 - t)

    def start_row(i):
        i2 = i % count
        back = i // count == 0
        s, r = i2 // 4, i2 % 4
        t = jnp.where(back, order(s), xor(q, s, nq))
        half = jnp.where(back, r // 2, r % 2)
        piece = jnp.where(back, r % 2, r // 2)
        core = jnp.where(back, (1 - c) * (1 - half) + c * half, c * (1 - half) + (1 - c) * half)
        return (2 * t + core) * local + piece * tile

    def load(i):
        return pltpu.make_async_copy(
            weight.at[pl.ds(pl.multiple_of(start_row(i), tile), tile), :],
            wbuf.at[i % BUFFERS], wsem.at[i % BUFFERS],
        )

    ins = [
        pltpu.make_async_copy(a, b, in_s.at[k])
        for k, (a, b) in enumerate(
            (
                (gain_hbm, gain), (x_hbm.at[:, 0:tile], xin.at[:, 0:tile]),
                (x_hbm.at[:, tile:local], xin.at[:, tile:local]), (cot_hbm, cot), (tenant_hbm, tenant),
                (down_hbm, down), (up_hbm, up), (drf_hbm, drf), (ucf_hbm, ucf),
            )
        )
    ]
    for k in range(5):
        ins[k].start()
    load(jnp.int32(0)).start()
    for k in range(5, 9):
        ins[k].start()
    for i in range(1, BUFFERS):
        load(jnp.int32(i)).start()

    barrier = pltpu.get_barrier_semaphore()

    def greet(**where):
        pl.semaphore_signal(barrier, inc=1, device_id=where, device_id_type=MESH)

    for k in range(1, ndp):
        greet(dp=(d + k) % ndp)
    greet(fsdp=mate)

    @pl.when(q + 1 < nq)
    def _():
        greet(fsdp=(f + 2) % n)

    @pl.when(q > 0)
    def _():
        greet(fsdp=(f + n - 2) % n)

    def ag_up(slot, p):
        return remote(ag.at[slot, p], ag.at[slot, p], ag_s.at[slot, p, 0], ag_r.at[slot, p], fsdp=(f + 2) % n)

    def ag_down(slot, p):
        return remote(ag.at[slot, p], ag.at[slot, p], ag_s.at[slot, p, 1], ag_r.at[slot, p], fsdp=(f + n - 2) % n)

    def ag_mate(slot, p):
        return remote(ag.at[slot, p], ag.at[slot, p], ag_sp.at[slot, p], ag_r.at[slot, p], fsdp=mate)

    def ag_own(p):
        @pl.when(q + 1 < nq)
        def _():
            ag_up(f, p).start()

        @pl.when(q > 0)
        def _():
            ag_down(f, p).start()

        ag_mate(f, p).start()

    def prepare(p, square):
        for j in range(p * tile // LANES, (p + 1) * tile // LANES):
            cols = slice(j * LANES, (j + 1) * LANES)
            xf = xin[:, cols].astype(F32)
            gained = (xf * gain[j : j + 1, :].astype(F32)).astype(BF16)
            square = square + xf * xf
            dpx[d, :, cols] = gained
            ag[f, p, :, j * LANES - p * tile : (j + 1) * LANES - p * tile] = gained
        return square

    ins[0].wait()
    ins[1].wait()
    square = prepare(0, jnp.zeros((rows, LANES), F32))
    pl.semaphore_wait(barrier, ndp + (q + 1 < nq).astype(jnp.int32) + (q > 0).astype(jnp.int32))
    ag_own(0)
    ins[2].wait()
    square = prepare(1, square)

    near, far = xor(d, 1, ndp), xor(d, 2, ndp)
    relayed = ndp == 4

    def dp_x(slot, to, k):
        return remote(dpx.at[slot], dpx.at[slot], dx_s.at[k], dx_r.at[slot], dp=to)

    def dp_g(slot, to, k):
        return remote(dpg.at[slot], dpg.at[slot], dg_s.at[k], dg_r.at[slot], dp=to)

    if relayed:
        dp_x(d, near, 0).start()
    ins[3].wait()
    ins[4].wait()
    alive = lax.broadcasted_iota(jnp.int32, (rows, LANES), 0) < live[0]
    for j in range(local // LANES):
        cols = slice(j * LANES, (j + 1) * LANES)
        kept = jnp.where(alive, cot[:, cols].astype(F32), 0.0).astype(BF16)
        grad[:, cols] = kept
        dpg[d, :, cols] = kept
    if relayed:
        dp_g(d, far, 0).start()
        dp_g(d, near, 1).start()
        dp_x(d, far, 1).start()
    else:
        for k in range(1, ndp):
            dp_x(d, (d + k) % ndp, k - 1).start()
            dp_g(d, (d + k) % ndp, k - 1).start()

    def relay():
        dp_x(near, far, 2).wait_recv()
        dp_x(near, far, 2).start()
        dp_g(far, near, 2).wait_recv()
        dp_g(far, near, 2).start()

    place_of = lax.broadcasted_iota(jnp.int32, (tenants * rank, rows), 0) // rank
    tenant_row = tenant[...]
    picked = place_of == tenant_row
    ins[5].wait()
    ins[6].wait()
    for at, lhs, rhs in ((0, down, dpx.at[d]), (1, up, grad)):
        full = lax.dot_general(lhs[...], rhs[...], NT, preferred_element_type=F32)
        full = jnp.where(picked, full, 0.0).reshape(tenants, rank, rows)
        pk[at, 0:rank, :] = jnp.sum(full, axis=0)
    power = jnp.sum(square.T, axis=0, keepdims=True)
    pk[0, rank : rank + 8, :] = jnp.broadcast_to(power, (8, rows))
    pk[1, rank : rank + 8, :] = jnp.zeros((8, rows), F32)

    pk_mate = remote(pk.at[1 - c], pkm, pk_s.at[0], pk_r.at[0], fsdp=mate)
    pk_mate.start()

    def pk_up():
        return remote(pksu, pku, pk_s.at[1], pk_r.at[1], fsdp=(f + 2) % n)

    def pk_down():
        return remote(pksd, pkd, pk_s.at[2], pk_r.at[2], fsdp=(f + n - 2) % n)

    def pk_back():
        return remote(pkt.at[c], pkt.at[c], pk_s.at[3], pk_r.at[3], fsdp=mate)

    def pk_spread():
        pk_mate.wait_recv()
        pkh[...] = pk[c] + pkm[...]

        @pl.when(q == 0)
        def _():
            pksu[...] = pkh[...]
            pk_up().start()

        @pl.when(q == nq - 1)
        def _():
            pksd[...] = pkh[...]
            pk_down().start()

    def pk_hop(j):
        @pl.when((q == j) & (q + 1 < nq))
        def _():
            pk_up().wait_recv()
            pksu[...] = pkh[...] + pku[...]
            pk_up().start()

        @pl.when((nq - 1 - q == j) & (q > 0))
        def _():
            pk_down().wait_recv()
            pksd[...] = pkh[...] + pkd[...]
            pk_down().start()

    def pk_sum():
        @pl.when(q == nq - 1)
        def _():
            pk_up().wait_recv()

        @pl.when(q == 0)
        def _():
            pk_down().wait_recv()

        below = jnp.where(q > 0, pku[...], 0.0)
        above = jnp.where(q + 1 < nq, pkd[...], 0.0)
        pkt[c] = pkh[...] + below + above
        pk_back().start()

    def sm_copy(k):
        return remote(sm, smrx.at[d], sm_s.at[k], sm_r.at[k], dp=(d + k) % ndp)

    def pk_use():
        pk_back().wait_recv()
        scale = lax.rsqrt(pkt[0, rank : rank + 1, :] / width + RMS_EPS)
        inner = pkt[0, 0:rank, :] * scale
        back = pkt[1, 0:rank, :]
        slot = jnp.zeros((1, rows), F32)
        for t in range(tenants):
            slot = jnp.where(tenant_row == t, slots[t].astype(F32), slot)
        sm[0:rank, :] = inner.astype(BF16)
        sm[rank : 2 * rank, :] = (back * scale).astype(BF16)
        sm[2 * rank :, :] = jnp.broadcast_to(slot, (16, rows)).astype(BF16)
        for k in range(1, ndp):
            sm_copy(k).start()
        smrx[d] = sm[...]
        spread_a[...] = jnp.where(picked, jnp.tile(inner, (tenants, 1)), 0.0).astype(BF16)
        spread_b[...] = jnp.where(picked, jnp.tile(back, (tenants, 1)), 0.0).astype(BF16)
        scale_col[...] = jnp.broadcast_to(scale, (rows, rows)).T

    def chain_copy(t, p, h, rsem, rx, to):
        part_of = pl.ds(h * (tile // 2), tile // 2)
        return remote(
            csend.at[t, p, part_of], rx.at[t, p, part_of], ch_s.at[t, p, h], rsem.at[t, p, h], fsdp=to
        )

    def chain_up(t, p, h):
        return chain_copy(t, p, h, up_r, uprx, (f + 2) % n)

    def chain_down(t, p, h):
        return chain_copy(t, p, h, dn_r, dnrx, (f + n - 2) % n)

    def send_up(t, p):
        chain_up(t, p, 0).start()

        @pl.when((t != q + 1) | (p == 0))
        def _():
            chain_up(t, p, 1).start()

    def send_down(t, p):
        chain_down(t, p, 0).start()

        @pl.when((t != q - 1) | (p == 0))
        def _():
            chain_down(t, p, 1).start()

    def mate_copy(t, p):
        return remote(psend.at[t, p], prx.at[t, p], pp_s.at[t, p], pp_r.at[t, p], fsdp=mate)

    def both(t, p):
        return part[t, p].astype(F32) + prx[t, p].astype(F32)

    def head(t):
        return ((t > q) & (q == 0)) | ((t < q) & (q == nq - 1))

    def chain_head(t, p):
        mate_copy(t, p).wait_recv()
        csend[t, p] = both(t, p).astype(BF16)

        @pl.when(t > q)
        def _():
            send_up(t, p)

        @pl.when(t < q)
        def _():
            send_down(t, p)

    def tick(j):
        k, p = (j + 1) // 2, (j + 1) % 2
        below, above = 2 * (q - k) + c, 2 * (q + k) + c
        pk_hop(j)

        @pl.when(q - k >= 0)
        def _():
            ag_up(below, p).wait_recv()

            @pl.when(q + 1 < nq)
            def _():
                ag_up(below, p).start()

            ag_mate(below, p).start()

        @pl.when(q + k < nq)
        def _():
            ag_down(above, p).wait_recv()

            @pl.when(q > 0)
            def _():
                ag_down(above, p).start()

            ag_mate(above, p).start()

        m = j - 1 - 2 * q

        @pl.when((q > 0) & (m >= 0) & (m < 2 * (nq - 1 - q)))
        def _():
            t, b = nq - 1 - m // 2, m % 2
            mate_copy(t, b).wait_recv()
            for h in range(2):
                chain_up(t, b, h).wait_recv()
            csend[t, b] = (both(t, b) + uprx[t, b].astype(F32)).astype(BF16)
            send_up(t, b)

        w = j - 1 - 2 * (nq - 1 - q)

        @pl.when((q < nq - 1) & (w >= 0) & (w < 2 * q))
        def _():
            t, b = w // 2, w % 2
            mate_copy(t, b).wait_recv()
            for h in range(2):
                chain_down(t, b, h).wait_recv()
            csend[t, b] = (both(t, b) + dnrx[t, b].astype(F32)).astype(BF16)
            send_down(t, b)

    period = max(TILES_PER_PIECE * rows // local, 3)
    ticks = 2 * (nq - 1)
    offset = -1
    chained = min(period * (nq - 1) + offset, count + 2 * nq)
    once = [(2, pk_spread), (2, lambda: ag_own(1)), (chained + 3, pk_sum), (chained + 5, pk_use)]
    if relayed:
        once.append((13, relay))

    def events(i, lo, hi):
        for at, what in once:
            if lo <= at < hi:
                pl.when(i == at)(what)
        j1, j2 = (i - offset) // period, (i - count) // 2 - 1
        hit1 = ((i - offset) % period == 0) & (j1 >= 1) & (j1 <= ticks) & (i <= count + 2 * (j1 + 1))
        hit2 = ((i - count) % 2 == 0) & (j2 >= 1) & (j2 <= ticks) & (i < period * j2 + offset)

        @pl.when(hit1 | hit2)
        def _():
            tick(jnp.where(hit1, j1, j2))

    @pl.loop(0, count)
    def _(i):
        events(i, 0, count)
        load(i).wait()
        s, r = i // 4, i % 4
        t, p = order(s), r % 2
        out = lax.dot_general(
            wbuf[i % BUFFERS], grad[...], NT, preferred_element_type=F32
        ).astype(BF16)
        load(i + BUFFERS).start()

        @pl.when(r < 2)
        def _():
            psend[t, p] = out
            mate_copy(t, p).start()

        @pl.when(r >= 2)
        def _():
            part[t, p] = out

        @pl.when((r == 3) & head(t))
        def _():
            chain_head(t, 0)
            chain_head(t, 1)

    acc[...] = jnp.zeros_like(acc)

    @pl.loop(count, 2 * count)
    def _(i):
        events(i, count, 2 * count)
        i2 = i - count
        s, r = i2 // 4, i2 % 4
        half, p = r % 2, r // 2
        t = xor(q, s, nq)
        slot = 2 * t + c * (1 - half) + (1 - c) * half

        @pl.when(half == 1)
        def _():
            ag_mate(slot, p).wait_recv()

        load(i).wait()
        acc[...] += jnp.dot(ag[slot, p], wbuf[i % BUFFERS], preferred_element_type=F32)

        @pl.when(i + BUFFERS < 2 * count)
        def _():
            load(i + BUFFERS).start()

    if relayed:
        corner = xor(d, 3, ndp)
        for slot in (far, corner):
            dp_x(slot, far, 0).wait_recv()
        for slot in (near, corner):
            dp_g(slot, near, 0).wait_recv()
    else:
        for k in range(1, ndp):
            dp_x((d + k) % ndp, (d + 1) % ndp, 0).wait_recv()
            dp_g((d + k) % ndp, (d + 1) % ndp, 0).wait_recv()
    for k in range(1, ndp):
        sm_copy(k).wait_recv()
    ins[7].wait()
    ins[8].wait()
    place = lax.broadcasted_iota(jnp.int32, (owned * rank, rows), 0) // rank + d * owned
    place = place.astype(F32)
    for at, src, dst, summed, old, line in (
        (rank, dpx, ga, row_a, drf, 0), (0, dpg, gb, col_b, ucf, owned * rank)
    ):
        lhs = jnp.concatenate(
            [
                jnp.where(
                    place == smrx[g, 2 * rank : 2 * rank + 1, :].astype(F32),
                    jnp.tile(smrx[g, at : at + rank, :].astype(F32), (owned, 1)),
                    0.0,
                ).astype(BF16)
                for g in range(ndp)
            ],
            axis=1,
        )
        step = min(512, local)
        for lo in range(0, local, step):
            rhs = src[:, :, lo : lo + step].reshape(ndp * rows, step)
            full = ADAPTER_SCALE * jnp.dot(lhs, rhs, preferred_element_type=F32)
            full = full.reshape(owned, rank, step)
            dst[:, :, lo : lo + step] = full
            sq = full * full + SQ_EPS
            summed[:, lo : lo + step] = BETA_TWO * old[:, lo : lo + step] + (1.0 - BETA_TWO) * (
                jnp.sum(sq, axis=1) / rank
            )
            flat = sq.reshape(owned * rank, step)
            total = flat[:, 0:LANES]
            for w in range(LANES, step, LANES):
                total = total + flat[:, w : w + LANES]
            here = slice(line, line + owned * rank)
            if lo == 0:
                lanes[here, :] = total
            else:
                lanes[here, :] += total
    cols = 2 * owned * rank
    st[...] = jnp.zeros_like(st)
    factor = drf[:, 0:LANES]
    for w in range(LANES, local, LANES):
        factor = factor + drf[:, w : w + LANES]
    lanes[cols:, :] = jnp.concatenate([factor, jnp.zeros((LANES - owned, LANES), F32)], axis=0)
    for k in range(cols // LANES + 1):
        st[k : k + 1, :] = jnp.sum(lanes[k * LANES : (k + 1) * LANES, :].T, axis=0, keepdims=True)

    def st_copy(k):
        return remote(st, strx.at[k], st_s.at[k], st_r.at[k], fsdp=(f + k) % n)

    for k in range(1, n):
        st_copy(k).start()

    @pl.when(q + 1 < nq)
    def _():
        chain_up(q + 1, 1, 1).start()

    @pl.when(q > 0)
    def _():
        chain_down(q - 1, 1, 1).start()
    chunk = min(512, local)
    for lo in range(0, local, chunk):
        here = slice(lo, lo + chunk)
        adapted = lax.dot_general(spread_a[...], up[:, here], TN, preferred_element_type=F32)
        wide = jnp.concatenate([scale_col[...]] * (chunk // rows), axis=1)
        projected[:, here] = (acc[:, here] * wide + ADAPTER_SCALE * adapted).astype(BF16)

    quarter = tile // 2
    for p in range(2):
        mate_copy(q, p).wait_recv()
        for h in range(2):
            here = slice(h * quarter, (h + 1) * quarter)
            there = slice(p * tile + h * quarter, p * tile + (h + 1) * quarter)
            out = lax.dot_general(down[:, there], spread_b[...], TN, preferred_element_type=F32)
            out = ADAPTER_SCALE * out + part[q, p, here, :].astype(F32) + prx[q, p, here, :].astype(F32)
            base[there, :] = out
    for p in range(2):
        for h in range(2):
            here = slice(h * quarter, (h + 1) * quarter)
            there = slice(p * tile + h * quarter, p * tile + (h + 1) * quarter)

            @pl.when(q > 0)
            def _():
                chain_up(q, p, h).wait_recv()

            @pl.when(q < nq - 1)
            def _():
                chain_down(q, p, h).wait_recv()

            from_up = jnp.where(q > 0, uprx[q, p, here, :].astype(F32), 0.0)
            from_dn = jnp.where(q < nq - 1, dnrx[q, p, here, :].astype(F32), 0.0)
            grad_t[there, :] = (base[there, :] + from_up + from_dn).astype(BF16)

    whole = st[...]
    for k in range(1, n):
        st_copy(k).wait_recv()
        whole = whole + strx[k]
    stats[...] = whole
    pk_mate.wait_send()
    pk_back().wait_send()

    @pl.when(q + 1 < nq)
    def _():
        pk_up().wait_send()

    @pl.when(q > 0)
    def _():
        pk_down().wait_send()

    for k in range(1, n):
        st_copy(k).wait_send()
    for k in range(1, ndp):
        sm_copy(k).wait_send()
        dp_x(d, (d + 1) % ndp, k - 1).wait_send()
        dp_g(d, (d + 1) % ndp, k - 1).wait_send()

    @pl.loop(0, nq)
    def _(t):
        slot = 2 * t + c
        for p in range(2):
            mate_copy(t, p).wait_send()

            @pl.when(t != q)
            def _():
                for h in range(2):
                    chain_up(t, p, h).wait_send()

            ag_mate(slot, p).wait_send()

            @pl.when((t <= q) & (q + 1 < nq))
            def _():
                ag_up(slot, p).wait_send()

            @pl.when((t >= q) & (q > 0))
            def _():
                ag_down(slot, p).wait_send()


def finish(
    rank, owned, width,
    projected, grad_t, ga, gb, row_a, col_b, stats, dcf, urf,
    projected_out, grad_t_out, update_a_out, update_b_out, row_a_out, col_a_out, row_b_out, col_b_out,
    update_a, update_b, col_a, row_b, sems, slot_sems,
):
    copies = [
        pltpu.make_async_copy(src, dst, sems.at[k])
        for k, (src, dst) in enumerate(
            (
                (projected, projected_out), (grad_t, grad_t_out), (row_a, row_a_out), (col_b, col_b_out),
                (col_a, col_a_out), (row_b, row_b_out),
            )
        )
    ]
    for k in range(4):
        copies[k].start()
    per = LANES // rank
    lines = owned // per
    sums = [
        jnp.concatenate(
            [
                stats[base + s // per : base + s // per + 1, s % per * rank : (s % per + 1) * rank]
                for s in range(owned)
            ],
            axis=0,
        )
        for base in (0, lines)
    ]
    new_a = BETA_TWO * dcf[...] + (1.0 - BETA_TWO) * (sums[0] / width)
    new_b = BETA_TWO * urf[...] + (1.0 - BETA_TWO) * (sums[1] / width)
    col_a[...] = new_a
    row_b[...] = new_b
    for k in (4, 5):
        copies[k].start()
    line = jnp.broadcast_to(stats[2 * lines : 2 * lines + 1, :], (owned, LANES))
    own = lax.broadcasted_iota(jnp.int32, (owned, LANES), 0) == lax.broadcasted_iota(
        jnp.int32, (owned, LANES), 1
    )
    kept = jnp.sum(jnp.where(own, line, 0.0), axis=1, keepdims=True)
    mean_a = (BETA_TWO * kept + (1.0 - BETA_TWO) * (jnp.sum(sums[0], axis=1, keepdims=True) / rank)) / width
    mean_b = jnp.sum(new_b, axis=1, keepdims=True) / rank
    wide_a = lax.rsqrt(row_a[...] / mean_a)
    wide_b = lax.rsqrt(col_b[...])
    tall_a = lax.rsqrt(new_a).T
    tall_b = lax.rsqrt(new_b / mean_b).T
    work = ((ga, update_a, update_a_out, wide_a, tall_a), (gb, update_b, update_b_out, wide_b, tall_b))
    for s in range(owned):
        for which, (src, dst, out, wide, tall) in enumerate(work):
            dst[s] = src[s] * wide[s : s + 1, :] * tall[:, s : s + 1]
            copy = pltpu.make_async_copy(dst.at[s], out.at[s], slot_sems.at[which, s])
            copy.start()
            copies.append(copy)
    for copy in copies:
        copy.wait()


def on_device(
    ndp,
    n,
    inputs,
    norm_gain_vector,
    weight,
    down_adapters,
    up_adapters,
    tenant,
    tenant_slot_index,
    live_row_count,
    cotangent,
    down_row_factor,
    down_column_factor,
    up_row_factor,
    up_column_factor,
):
    rows, local = inputs.shape
    width = weight.shape[0]
    tenants, rank = down_adapters.shape[1:]
    owned = down_row_factor.shape[0]
    down = jnp.transpose(down_adapters, (1, 2, 0)).reshape(tenants * rank, local)
    up = up_adapters.reshape(tenants * rank, local)
    gain = norm_gain_vector.reshape(local // LANES, LANES)
    tile = local // 2
    nq = n // 2
    cols = 2 * owned * rank
    dma = pltpu.SemaphoreType.DMA
    piece = pltpu.VMEM((nq, 2, tile, rows), BF16)
    anywhere = pl.BlockSpec(memory_space=pl.ANY)
    vmem = pl.BlockSpec(memory_space=pltpu.VMEM)
    scalar = pl.BlockSpec(memory_space=pltpu.SMEM)
    small = pltpu.VMEM((rank + 8, rows), F32)
    results = (
        ((rows, local), BF16),
        ((local, rows), BF16),
        ((owned, rank, local), F32),
        ((owned, rank, local), F32),
        ((owned, local), F32),
        ((owned, local), F32),
        ((8, LANES), F32),
    )
    projected, grad_t, ga, gb, row_a, col_b, stats = pl.pallas_call(
        functools.partial(kernel, ndp, n, rank, tenants, owned, width),
        out_shape=tuple(pltpu.VMEM(*r) for r in results),
        in_specs=[scalar] * 2 + [anywhere] * 9,
        out_specs=(vmem,) * 7,
        scratch_shapes=[
            pltpu.VMEM((BUFFERS, tile, local), BF16),
            pltpu.VMEM((n, 2, rows, tile), BF16),
            pltpu.VMEM((ndp, rows, local), BF16),
            pltpu.VMEM((ndp, rows, local), BF16),
            pltpu.VMEM((rows, local), BF16),
            pltpu.VMEM((rows, local), F32),
            piece, piece, piece, piece, piece, piece,
            pltpu.VMEM((rows, local), BF16),
            pltpu.VMEM((rows, local), BF16),
            pltpu.VMEM((local // LANES, LANES), BF16),
            pltpu.VMEM((1, rows), jnp.int32),
            pltpu.VMEM((owned, local), F32),
            pltpu.VMEM((owned, local), F32),
            pltpu.VMEM((tenants * rank, local), BF16),
            pltpu.VMEM((tenants * rank, local), BF16),
            pltpu.VMEM((2, rank + 8, rows), F32),
            small, small, small, small, small, small,
            pltpu.VMEM((2, rank + 8, rows), F32),
            pltpu.VMEM((2 * rank + 16, rows), BF16),
            pltpu.VMEM((ndp, 2 * rank + 16, rows), BF16),
            pltpu.VMEM((8, LANES), F32),
            pltpu.VMEM((n, 8, LANES), F32),
            pltpu.VMEM((tenants * rank, rows), BF16),
            pltpu.VMEM((tenants * rank, rows), BF16),
            pltpu.VMEM((cols + LANES, LANES), F32),
            pltpu.VMEM((rows, rows), F32),
            pltpu.VMEM((local, rows), F32),
        ]
        + [
            dma((BUFFERS,)),
            dma((9,)),
            dma((n, 2, 2)),
            dma((n, 2)),
            dma((n, 2)),
            dma((ndp,)),
            dma((ndp,)),
            dma((ndp,)),
            dma((ndp,)),
            dma((ndp,)),
            dma((ndp,)),
            dma((nq, 2)),
            dma((nq, 2)),
            dma((nq, 2, 2)),
            dma((nq, 2, 2)),
            dma((nq, 2, 2)),
            dma((4,)),
            dma((4,)),
            dma((n,)),
            dma((n,)),
        ],
        compiler_params=pltpu.CompilerParams(
            collective_id=0, has_side_effects=True, vmem_limit_bytes=54 * 1024 * 1024
        ),
    )(
        tenant_slot_index, live_row_count, inputs, gain, cotangent, tenant.reshape(1, rows),
        down_row_factor, up_column_factor, down, up, weight,
    )

    shapes = (
        ((rows, local), BF16),
        ((local, rows), BF16),
        ((owned, rank, local), F32),
        ((owned, rank, local), F32),
        ((owned, local), F32),
        ((owned, rank), F32),
        ((owned, rank), F32),
        ((owned, local), F32),
    )
    outs = pl.pallas_call(
        functools.partial(finish, rank, owned, width),
        out_shape=tuple(jax.ShapeDtypeStruct(*r) for r in shapes),
        in_specs=[vmem] * 9,
        out_specs=(anywhere,) * 8,
        scratch_shapes=[
            pltpu.VMEM((owned, rank, local), F32),
            pltpu.VMEM((owned, rank, local), F32),
            pltpu.VMEM((owned, rank), F32),
            pltpu.VMEM((owned, rank), F32),
            dma((6,)),
            dma((2, owned)),
        ],
        compiler_params=pltpu.CompilerParams(vmem_limit_bytes=16 * 1024 * 1024),
    )(projected, grad_t, ga, gb, row_a, col_b, stats, down_column_factor, up_row_factor)
    return outs[:2] + (jnp.swapaxes(outs[2], 1, 2),) + outs[3:]


def solution(mesh):
    return jax.shard_map(
        functools.partial(on_device, mesh.shape["dp"], mesh.shape["fsdp"]),
        mesh=mesh,
        in_specs=(
            P("dp", "fsdp"),
            P("fsdp"),
            P(None, "fsdp"),
            P("fsdp", None, None),
            P(None, None, "fsdp"),
            P("dp"),
            P(),
            P("dp"),
            P("dp", "fsdp"),
            P("dp", "fsdp"),
            P("dp", None),
            P("dp", None),
            P("dp", "fsdp"),
        ),
        out_specs=(
            P("dp", "fsdp"),
            P("fsdp", "dp"),
            P("dp", "fsdp", None),
            P("dp", None, "fsdp"),
            P("dp", "fsdp"),
            P("dp", None),
            P("dp", None),
            P("dp", "fsdp"),
        ),
        check_vma=False,
    )
```

```python
import functools

import jax
import jax.numpy as jnp
from jax import lax
from jax.experimental import pallas as pl
from jax.experimental.pallas import tpu as pltpu
from jax.sharding import PartitionSpec as P

ADAPTER_SCALE = 0.5
BETA_TWO = 0.9
SQ_EPS = 1e-30
RMS_EPS = 1e-05
BUFFERS = 5
LANES = 128
TILES_PER_PIECE = 80
LEAD = 2.5
SHARED_COST = 1.7
NT = (((1,), (1,)), ((), ()))
TN = (((0,), (0,)), ((), ()))
F32, BF16 = jnp.float32, jnp.bfloat16
MESH = pl.DeviceIdType.MESH


def xor(a, b, count):
    out, bit = 0, 1
    while bit < count:
        out = out + ((a // bit + b // bit) % 2) * bit
        bit *= 2
    return out


def kernel(
    ndp, n, rank, tenants, owned, width,
    slots, live, x_hbm, gain_hbm, cot_hbm, tenant_hbm, drf_hbm, ucf_hbm, down_hbm, up_hbm, weight,
    projected, grad_t, ga, gb, row_a, col_b, stats,
    wbuf, ag, dpx, dpg, grad, gradt, acc, part, psend, prx, csend, uprx, dnrx,
    xin, cot, gain, tenant, drf, ucf, down, up,
    pk, pkm, pkh, pksu, pksd, pku, pkd, pkt, sm, smrx, st, strx, spread_a, spread_b, lanes, scale_col, base, adapted,
    wsem, in_s, ag_s, ag_sp, ag_r, dx_s, dx_r, dg_s, dg_r, sm_s, sm_r, pp_s, pp_r, ch_s, up_r, dn_r,
    pk_s, pk_r, st_s, st_r,
):
    rows, local = xin.shape
    tile = local // 2
    nq = n // 2
    shared = min(2, nq)
    first, count = 4 * (nq - shared), 4 * nq
    total = count + first
    d = lax.axis_index("dp")
    f = lax.axis_index("fsdp")
    q, c = f // 2, f % 2
    mate = 2 * q + 1 - c

    def remote(src, dst, ssem, rsem, **where):
        return pltpu.make_async_remote_copy(
            src_ref=src, dst_ref=dst, send_sem=ssem, recv_sem=rsem,
            device_id=where, device_id_type=MESH,
        )

    def order(s):
        low = q < nq // 2
        at = jnp.where(low, q, nq - 1 - q)
        t = jnp.where(s < nq - 1 - at, nq - 1 - s, s - (nq - 1 - at))
        return jnp.where(low, t, nq - 1 - t)

    def block(i):
        back = i < count
        i2 = jnp.where(back, i, i - count)
        r = i2 % 4
        t = order(jnp.where(back, i2 // 4, nq - shared - 1 - i2 // 4))
        half, p = r % 2, r // 2
        core = jnp.where(back, (1 - c) * (1 - half) + c * half, c * (1 - half) + (1 - c) * half)
        return t, half, p, core

    def start_row(i):
        t, _, p, core = block(i)
        return (2 * t + core) * local + p * tile

    def load(i):
        return pltpu.make_async_copy(
            weight.at[pl.ds(pl.multiple_of(start_row(i), tile), tile), :],
            wbuf.at[i % BUFFERS], wsem.at[i % BUFFERS],
        )

    ins = [
        pltpu.make_async_copy(a, b, in_s.at[k])
        for k, (a, b) in enumerate(
            (
                (gain_hbm, gain), (x_hbm.at[:, 0:tile], xin.at[:, 0:tile]),
                (x_hbm.at[:, tile:local], xin.at[:, tile:local]), (cot_hbm, cot), (tenant_hbm, tenant),
                (down_hbm, down), (up_hbm, up), (drf_hbm, drf), (ucf_hbm, ucf),
            )
        )
    ]
    for k in range(7):
        ins[k].start()
    for i in range(BUFFERS):
        load(jnp.int32(i)).start()
    for k in range(7, 9):
        ins[k].start()

    barrier = pltpu.get_barrier_semaphore()

    def greet(**where):
        pl.semaphore_signal(barrier, inc=1, device_id=where, device_id_type=MESH)

    for k in range(1, ndp):
        greet(dp=(d + k) % ndp)
    greet(fsdp=mate)

    @pl.when(q + 1 < nq)
    def _():
        greet(fsdp=(f + 2) % n)

    @pl.when(q > 0)
    def _():
        greet(fsdp=(f + n - 2) % n)

    def ag_up(slot, p):
        return remote(ag.at[slot, p], ag.at[slot, p], ag_s.at[slot, p, 0], ag_r.at[slot, p], fsdp=(f + 2) % n)

    def ag_down(slot, p):
        return remote(ag.at[slot, p], ag.at[slot, p], ag_s.at[slot, p, 1], ag_r.at[slot, p], fsdp=(f + n - 2) % n)

    def ag_mate(slot, p):
        return remote(ag.at[slot, p], ag.at[slot, p], ag_sp.at[slot, p], ag_r.at[slot, p], fsdp=mate)

    def ag_own(p):
        @pl.when(q + 1 < nq)
        def _():
            ag_up(f, p).start()

        @pl.when(q > 0)
        def _():
            ag_down(f, p).start()

        ag_mate(f, p).start()

    def prepare(p, square):
        for j in range(p * tile // LANES, (p + 1) * tile // LANES):
            cols = slice(j * LANES, (j + 1) * LANES)
            xf = xin[:, cols].astype(F32)
            gained = (xf * gain[j : j + 1, :].astype(F32)).astype(BF16)
            square = square + xf * xf
            dpx[d, :, cols] = gained
            ag[f, p, :, j * LANES - p * tile : (j + 1) * LANES - p * tile] = gained
        return square

    ins[0].wait()
    ins[1].wait()
    square = prepare(0, jnp.zeros((rows, LANES), F32))
    pl.semaphore_wait(barrier, ndp + (q + 1 < nq).astype(jnp.int32) + (q > 0).astype(jnp.int32))
    ag_own(0)
    ins[2].wait()
    square = prepare(1, square)

    near, far = xor(d, 1, ndp), xor(d, 2, ndp)
    relayed = ndp == 4

    def dp_x(slot, to, k):
        return remote(dpx.at[slot], dpx.at[slot], dx_s.at[k], dx_r.at[slot], dp=to)

    def dp_g(slot, to, k):
        return remote(dpg.at[slot], dpg.at[slot], dg_s.at[k], dg_r.at[slot], dp=to)

    if relayed:
        dp_x(d, near, 0).start()
    ins[3].wait()
    ins[4].wait()
    alive = lax.broadcasted_iota(jnp.int32, (rows, LANES), 0) < live[0]
    for j in range(local // LANES):
        cols = slice(j * LANES, (j + 1) * LANES)
        kept = jnp.where(alive, cot[:, cols].astype(F32), 0.0)
        gradt[cols, :] = kept.T.astype(BF16)
        kept = kept.astype(BF16)
        grad[:, cols] = kept
        dpg[d, :, cols] = kept
    if relayed:
        dp_g(d, far, 0).start()
        dp_g(d, near, 1).start()
        dp_x(d, far, 1).start()
    else:
        for k in range(1, ndp):
            dp_x(d, (d + k) % ndp, k - 1).start()
            dp_g(d, (d + k) % ndp, k - 1).start()

    def relay():
        dp_x(near, far, 2).wait_recv()
        dp_x(near, far, 2).start()
        dp_g(far, near, 2).wait_recv()
        dp_g(far, near, 2).start()

    place_of = lax.broadcasted_iota(jnp.int32, (tenants * rank, rows), 0) // rank
    tenant_row = tenant[...]
    picked = place_of == tenant_row
    ins[5].wait()
    ins[6].wait()
    for at, lhs, rhs in ((0, down, dpx.at[d]), (1, up, grad)):
        full = lax.dot_general(lhs[...], rhs[...], NT, preferred_element_type=F32)
        full = jnp.where(picked, full, 0.0).reshape(tenants, rank, rows)
        pk[at, 0:rank, :] = jnp.sum(full, axis=0)
    power = jnp.sum(square.T, axis=0, keepdims=True)
    pk[0, rank : rank + 8, :] = jnp.broadcast_to(power, (8, rows))
    pk[1, rank : rank + 8, :] = jnp.zeros((8, rows), F32)

    pk_mate = remote(pk.at[1 - c], pkm, pk_s.at[0], pk_r.at[0], fsdp=mate)
    pk_mate.start()

    def pk_up():
        return remote(pksu, pku, pk_s.at[1], pk_r.at[1], fsdp=(f + 2) % n)

    def pk_down():
        return remote(pksd, pkd, pk_s.at[2], pk_r.at[2], fsdp=(f + n - 2) % n)

    def pk_back():
        return remote(pkt.at[c], pkt.at[c], pk_s.at[3], pk_r.at[3], fsdp=mate)

    def pk_spread():
        pk_mate.wait_recv()
        pkh[...] = pk[c] + pkm[...]

        @pl.when(q == 0)
        def _():
            pksu[...] = pkh[...]
            pk_up().start()

        @pl.when(q == nq - 1)
        def _():
            pksd[...] = pkh[...]
            pk_down().start()

    def pk_hop(j):
        @pl.when((q == j) & (q + 1 < nq))
        def _():
            pk_up().wait_recv()
            pksu[...] = pkh[...] + pku[...]
            pk_up().start()

        @pl.when((nq - 1 - q == j) & (q > 0))
        def _():
            pk_down().wait_recv()
            pksd[...] = pkh[...] + pkd[...]
            pk_down().start()

    def pk_sum():
        @pl.when(q == nq - 1)
        def _():
            pk_up().wait_recv()

        @pl.when(q == 0)
        def _():
            pk_down().wait_recv()

        below = jnp.where(q > 0, pku[...], 0.0)
        above = jnp.where(q + 1 < nq, pkd[...], 0.0)
        pkt[c] = pkh[...] + below + above
        pk_back().start()

    def sm_copy(k):
        return remote(sm, smrx.at[d], sm_s.at[k], sm_r.at[k], dp=(d + k) % ndp)

    def pk_use():
        pk_back().wait_recv()
        scale = lax.rsqrt(pkt[0, rank : rank + 1, :] / width + RMS_EPS)
        inner = pkt[0, 0:rank, :] * scale
        back = pkt[1, 0:rank, :]
        slot = jnp.zeros((1, rows), F32)
        for t in range(tenants):
            slot = jnp.where(tenant_row == t, slots[t].astype(F32), slot)
        sm[0:rank, :] = inner.astype(BF16)
        sm[rank : 2 * rank, :] = (back * scale).astype(BF16)
        sm[2 * rank :, :] = jnp.broadcast_to(slot, (16, rows)).astype(BF16)
        for k in range(1, ndp):
            sm_copy(k).start()
        smrx[d] = sm[...]
        spread_a[...] = jnp.where(picked, jnp.tile(inner, (tenants, 1)), 0.0).astype(BF16)
        spread_b[...] = jnp.where(picked, jnp.tile(back, (tenants, 1)), 0.0).astype(BF16)
        scale_col[...] = jnp.broadcast_to(scale, (rows, rows)).T

    def chain_copy(t, p, h, rsem, rx, to):
        part_of = pl.ds(h * (tile // 2), tile // 2)
        return remote(
            csend.at[t, p, part_of], rx.at[t, p, part_of], ch_s.at[t, p, h], rsem.at[t, p, h], fsdp=to
        )

    def chain_up(t, p, h):
        return chain_copy(t, p, h, up_r, uprx, (f + 2) % n)

    def chain_down(t, p, h):
        return chain_copy(t, p, h, dn_r, dnrx, (f + n - 2) % n)

    def send_up(t, p):
        chain_up(t, p, 0).start()

        @pl.when((t != q + 1) | (p == 0))
        def _():
            chain_up(t, p, 1).start()

    def send_down(t, p):
        chain_down(t, p, 0).start()

        @pl.when((t != q - 1) | (p == 0))
        def _():
            chain_down(t, p, 1).start()

    def mate_copy(t, p):
        return remote(psend.at[t, p], prx.at[t, p], pp_s.at[t, p], pp_r.at[t, p], fsdp=mate)

    def both(t, p):
        return part[t, p].astype(F32) + prx[t, p].astype(F32)

    def head(t):
        return ((t > q) & (q == 0)) | ((t < q) & (q == nq - 1))

    def chain_head(t, p):
        mate_copy(t, p).wait_recv()
        csend[t, p] = both(t, p).astype(BF16)

        @pl.when(t > q)
        def _():
            send_up(t, p)

        @pl.when(t < q)
        def _():
            send_down(t, p)

    def tick(j):
        k, p = (j + 1) // 2, (j + 1) % 2
        below, above = 2 * (q - k) + c, 2 * (q + k) + c
        pk_hop(j)

        @pl.when(q - k >= 0)
        def _():
            ag_up(below, p).wait_recv()

            @pl.when(q + 1 < nq)
            def _():
                ag_up(below, p).start()

            ag_mate(below, p).start()

        @pl.when(q + k < nq)
        def _():
            ag_down(above, p).wait_recv()

            @pl.when(q > 0)
            def _():
                ag_down(above, p).start()

            ag_mate(above, p).start()

        m = j - 1 - 2 * q

        @pl.when((q > 0) & (m >= 0) & (m < 2 * (nq - 1 - q)))
        def _():
            t, b = nq - 1 - m // 2, m % 2
            mate_copy(t, b).wait_recv()
            for h in range(2):
                chain_up(t, b, h).wait_recv()
            csend[t, b] = (both(t, b) + uprx[t, b].astype(F32)).astype(BF16)
            send_up(t, b)

        w = j - 1 - 2 * (nq - 1 - q)

        @pl.when((q < nq - 1) & (w >= 0) & (w < 2 * q))
        def _():
            t, b = w // 2, w % 2
            mate_copy(t, b).wait_recv()
            for h in range(2):
                chain_down(t, b, h).wait_recv()
            csend[t, b] = (both(t, b) + dnrx[t, b].astype(F32)).astype(BF16)
            send_down(t, b)

    def adapter_base():
        chunk = min(512, local)
        for lo in range(0, local, chunk):
            here = slice(lo, lo + chunk)
            adapted[:, here] = ADAPTER_SCALE * lax.dot_general(
                spread_a[...], up[:, here], TN, preferred_element_type=F32
            )

    def gradient_base():
        for p in range(2):
            mate_copy(q, p).wait_recv()
            for h in range(2):
                here = slice(h * quarter, (h + 1) * quarter)
                there = slice(p * tile + h * quarter, p * tile + (h + 1) * quarter)
                out = lax.dot_general(down[:, there], spread_b[...], TN, preferred_element_type=F32)
                out = ADAPTER_SCALE * out + part[q, p, here, :].astype(F32) + prx[q, p, here, :].astype(F32)
                base[there, :] = out

    quarter = tile // 2
    period = max(TILES_PER_PIECE * rows // local, 3)
    ticks = 2 * (nq - 1)
    spent, at, when = 0.0, 0, []
    for j in range(1, ticks + 1):
        while spent < period * j - LEAD and at < total:
            spent += SHARED_COST if first <= at < count else 1.0
            at += 1
        when.append(at)
    for j in range(ticks, 0, -1):
        needed = count + 2 * j - 6 if j > 2 else count + 2 * j - 10
        later = when[j] - 1 if j < ticks else total - 1
        when[j - 1] = max(min(when[j - 1], needed, later), 2 * j)
    chained = when[nq - 2]
    once = [(2, pk_spread), (2, lambda: ag_own(1)), (chained + 2, pk_sum), (chained + 4, pk_use)]
    once += [(total - 4, adapter_base), (total - 3, gradient_base)]
    if relayed:
        once.append((first + 2, relay))

    def events(i, lo, hi):
        for at, what in once:
            if lo <= at < hi:
                pl.when(i == at)(what)
        j = jnp.int32(0)
        for k, at in enumerate(when):
            if lo <= at < hi:
                j = jnp.where(i == at, k + 1, j)
        if any(lo <= at < hi for at in when):
            pl.when(j > 0)(lambda: tick(j))

    def backward(i):
        t, half, p, _ = block(i)
        out = jnp.dot(wbuf[i % BUFFERS], gradt[...], preferred_element_type=F32).astype(BF16)

        @pl.when(half == 0)
        def _():
            psend[t, p] = out
            mate_copy(t, p).start()

        @pl.when(half == 1)
        def _():
            part[t, p] = out

        @pl.when((i % 4 == 3) & head(t))
        def _():
            chain_head(t, 0)
            chain_head(t, 1)

    def forward(i):
        t, _, p, core = block(i)
        slot = 2 * t + core

        @pl.when(core != c)
        def _():
            ag_mate(slot, p).wait_recv()

        acc[...] += jnp.dot(ag[slot, p], wbuf[i % BUFFERS], preferred_element_type=F32)

    def refill(i):
        @pl.when(i + BUFFERS < total)
        def _():
            load(i + BUFFERS).start()

    @pl.loop(0, first)
    def _(i):
        events(i, 0, first)
        load(i).wait()
        backward(i)
        refill(i)

    acc[...] = jnp.zeros_like(acc)

    @pl.loop(first, count)
    def _(i):
        events(i, first, count)
        load(i).wait()
        backward(i)

        @pl.when(i >= 0)
        def _():
            forward(i)

        refill(i)

    @pl.loop(count, total)
    def _(i):
        events(i, count, total)
        load(i).wait()
        forward(i)
        refill(i)

    if relayed:
        corner = xor(d, 3, ndp)
        for slot in (far, corner):
            dp_x(slot, far, 0).wait_recv()
        for slot in (near, corner):
            dp_g(slot, near, 0).wait_recv()
    else:
        for k in range(1, ndp):
            dp_x((d + k) % ndp, (d + 1) % ndp, 0).wait_recv()
            dp_g((d + k) % ndp, (d + 1) % ndp, 0).wait_recv()
    for k in range(1, ndp):
        sm_copy(k).wait_recv()
    ins[7].wait()
    ins[8].wait()
    place = lax.broadcasted_iota(jnp.int32, (owned * rank, rows), 0) // rank + d * owned
    place = place.astype(F32)
    for at, src, dst, summed, old, line in (
        (rank, dpx, ga, row_a, drf, 0), (0, dpg, gb, col_b, ucf, owned * rank)
    ):
        lhs = jnp.concatenate(
            [
                jnp.where(
                    place == smrx[g, 2 * rank : 2 * rank + 1, :].astype(F32),
                    jnp.tile(smrx[g, at : at + rank, :].astype(F32), (owned, 1)),
                    0.0,
                ).astype(BF16)
                for g in range(ndp)
            ],
            axis=1,
        )
        step = min(512, local)
        for lo in range(0, local, step):
            rhs = src[:, :, lo : lo + step].reshape(ndp * rows, step)
            full = ADAPTER_SCALE * jnp.dot(lhs, rhs, preferred_element_type=F32)
            full = full.reshape(owned, rank, step)
            dst[:, :, lo : lo + step] = full
            sq = full * full + SQ_EPS
            summed[:, lo : lo + step] = BETA_TWO * old[:, lo : lo + step] + (1.0 - BETA_TWO) * (
                jnp.sum(sq, axis=1) / rank
            )
            flat = sq.reshape(owned * rank, step)
            summed_up = flat[:, 0:LANES]
            for w in range(LANES, step, LANES):
                summed_up = summed_up + flat[:, w : w + LANES]
            here = slice(line, line + owned * rank)
            if lo == 0:
                lanes[here, :] = summed_up
            else:
                lanes[here, :] += summed_up
    cols = 2 * owned * rank
    st[...] = jnp.zeros_like(st)
    factor = drf[:, 0:LANES]
    for w in range(LANES, local, LANES):
        factor = factor + drf[:, w : w + LANES]
    lanes[cols:, :] = jnp.concatenate([factor, jnp.zeros((LANES - owned, LANES), F32)], axis=0)
    for k in range(cols // LANES + 1):
        st[k : k + 1, :] = jnp.sum(lanes[k * LANES : (k + 1) * LANES, :].T, axis=0, keepdims=True)

    def st_copy(k):
        return remote(st, strx.at[k], st_s.at[k], st_r.at[k], fsdp=(f + k) % n)

    for k in range(1, n):
        st_copy(k).start()

    @pl.when(q + 1 < nq)
    def _():
        chain_up(q + 1, 1, 1).start()

    @pl.when(q > 0)
    def _():
        chain_down(q - 1, 1, 1).start()
    wide = jnp.concatenate([scale_col[...]] * (local // rows), axis=1)
    projected[...] = (acc[...] * wide + adapted[...]).astype(BF16)
    for p in range(2):
        for h in range(2):
            here = slice(h * quarter, (h + 1) * quarter)
            there = slice(p * tile + h * quarter, p * tile + (h + 1) * quarter)

            @pl.when(q > 0)
            def _():
                chain_up(q, p, h).wait_recv()

            @pl.when(q < nq - 1)
            def _():
                chain_down(q, p, h).wait_recv()

            from_up = jnp.where(q > 0, uprx[q, p, here, :].astype(F32), 0.0)
            from_dn = jnp.where(q < nq - 1, dnrx[q, p, here, :].astype(F32), 0.0)
            grad_t[there, :] = (base[there, :] + from_up + from_dn).astype(BF16)

    whole = st[...]
    for k in range(1, n):
        st_copy(k).wait_recv()
        whole = whole + strx[k]
    stats[...] = whole
    pk_mate.wait_send()
    pk_back().wait_send()

    @pl.when(q + 1 < nq)
    def _():
        pk_up().wait_send()

    @pl.when(q > 0)
    def _():
        pk_down().wait_send()

    for k in range(1, n):
        st_copy(k).wait_send()
    for k in range(1, ndp):
        sm_copy(k).wait_send()
        dp_x(d, (d + 1) % ndp, k - 1).wait_send()
        dp_g(d, (d + 1) % ndp, k - 1).wait_send()

    @pl.loop(0, nq)
    def _(t):
        slot = 2 * t + c
        for p in range(2):
            mate_copy(t, p).wait_send()

            @pl.when(t != q)
            def _():
                for h in range(2):
                    chain_up(t, p, h).wait_send()

            ag_mate(slot, p).wait_send()

            @pl.when((t <= q) & (q + 1 < nq))
            def _():
                ag_up(slot, p).wait_send()

            @pl.when((t >= q) & (q > 0))
            def _():
                ag_down(slot, p).wait_send()


def finish(
    rank, owned, width,
    projected, grad_t, ga, gb, row_a, col_b, stats, dcf, urf,
    projected_out, grad_t_out, update_a_out, update_b_out, row_a_out, col_a_out, row_b_out, col_b_out,
    update_a, update_b, col_a, row_b, sems, slot_sems,
):
    copies = [
        pltpu.make_async_copy(src, dst, sems.at[k])
        for k, (src, dst) in enumerate(
            (
                (projected, projected_out), (grad_t, grad_t_out), (row_a, row_a_out), (col_b, col_b_out),
                (col_a, col_a_out), (row_b, row_b_out),
            )
        )
    ]
    for k in range(4):
        copies[k].start()
    per = LANES // rank
    lines = owned // per
    sums = [
        jnp.concatenate(
            [
                stats[base + s // per : base + s // per + 1, s % per * rank : (s % per + 1) * rank]
                for s in range(owned)
            ],
            axis=0,
        )
        for base in (0, lines)
    ]
    new_a = BETA_TWO * dcf[...] + (1.0 - BETA_TWO) * (sums[0] / width)
    new_b = BETA_TWO * urf[...] + (1.0 - BETA_TWO) * (sums[1] / width)
    col_a[...] = new_a
    row_b[...] = new_b
    for k in (4, 5):
        copies[k].start()
    line = jnp.broadcast_to(stats[2 * lines : 2 * lines + 1, :], (owned, LANES))
    own = lax.broadcasted_iota(jnp.int32, (owned, LANES), 0) == lax.broadcasted_iota(
        jnp.int32, (owned, LANES), 1
    )
    kept = jnp.sum(jnp.where(own, line, 0.0), axis=1, keepdims=True)
    mean_a = (BETA_TWO * kept + (1.0 - BETA_TWO) * (jnp.sum(sums[0], axis=1, keepdims=True) / rank)) / width
    mean_b = jnp.sum(new_b, axis=1, keepdims=True) / rank
    wide_a = lax.rsqrt(row_a[...] / mean_a)
    wide_b = lax.rsqrt(col_b[...])
    tall_a = lax.rsqrt(new_a).T
    tall_b = lax.rsqrt(new_b / mean_b).T
    work = ((ga, update_a, update_a_out, wide_a, tall_a), (gb, update_b, update_b_out, wide_b, tall_b))
    for s in range(owned):
        for which, (src, dst, out, wide, tall) in enumerate(work):
            dst[s] = src[s] * wide[s : s + 1, :] * tall[:, s : s + 1]
            copy = pltpu.make_async_copy(dst.at[s], out.at[s], slot_sems.at[which, s])
            copy.start()
            copies.append(copy)
    for copy in copies:
        copy.wait()


def on_device(
    ndp,
    n,
    inputs,
    norm_gain_vector,
    weight,
    down_adapters,
    up_adapters,
    tenant,
    tenant_slot_index,
    live_row_count,
    cotangent,
    down_row_factor,
    down_column_factor,
    up_row_factor,
    up_column_factor,
):
    rows, local = inputs.shape
    width = weight.shape[0]
    tenants, rank = down_adapters.shape[1:]
    owned = down_row_factor.shape[0]
    down = jnp.transpose(down_adapters, (1, 2, 0)).reshape(tenants * rank, local)
    up = up_adapters.reshape(tenants * rank, local)
    gain = norm_gain_vector.reshape(local // LANES, LANES)
    tile = local // 2
    nq = n // 2
    cols = 2 * owned * rank
    dma = pltpu.SemaphoreType.DMA
    piece = pltpu.VMEM((nq, 2, tile, rows), BF16)
    anywhere = pl.BlockSpec(memory_space=pl.ANY)
    vmem = pl.BlockSpec(memory_space=pltpu.VMEM)
    scalar = pl.BlockSpec(memory_space=pltpu.SMEM)
    small = pltpu.VMEM((rank + 8, rows), F32)
    results = (
        ((rows, local), BF16),
        ((local, rows), BF16),
        ((owned, rank, local), F32),
        ((owned, rank, local), F32),
        ((owned, local), F32),
        ((owned, local), F32),
        ((8, LANES), F32),
    )
    projected, grad_t, ga, gb, row_a, col_b, stats = pl.pallas_call(
        functools.partial(kernel, ndp, n, rank, tenants, owned, width),
        out_shape=tuple(pltpu.VMEM(*r) for r in results),
        in_specs=[scalar] * 2 + [anywhere] * 9,
        out_specs=(vmem,) * 7,
        scratch_shapes=[
            pltpu.VMEM((BUFFERS, tile, local), BF16),
            pltpu.VMEM((n, 2, rows, tile), BF16),
            pltpu.VMEM((ndp, rows, local), BF16),
            pltpu.VMEM((ndp, rows, local), BF16),
            pltpu.VMEM((rows, local), BF16),
            pltpu.VMEM((local, rows), BF16),
            pltpu.VMEM((rows, local), F32),
            piece, piece, piece, piece, piece, piece,
            pltpu.VMEM((rows, local), BF16),
            pltpu.VMEM((rows, local), BF16),
            pltpu.VMEM((local // LANES, LANES), BF16),
            pltpu.VMEM((1, rows), jnp.int32),
            pltpu.VMEM((owned, local), F32),
            pltpu.VMEM((owned, local), F32),
            pltpu.VMEM((tenants * rank, local), BF16),
            pltpu.VMEM((tenants * rank, local), BF16),
            pltpu.VMEM((2, rank + 8, rows), F32),
            small, small, small, small, small, small,
            pltpu.VMEM((2, rank + 8, rows), F32),
            pltpu.VMEM((2 * rank + 16, rows), BF16),
            pltpu.VMEM((ndp, 2 * rank + 16, rows), BF16),
            pltpu.VMEM((8, LANES), F32),
            pltpu.VMEM((n, 8, LANES), F32),
            pltpu.VMEM((tenants * rank, rows), BF16),
            pltpu.VMEM((tenants * rank, rows), BF16),
            pltpu.VMEM((cols + LANES, LANES), F32),
            pltpu.VMEM((rows, rows), F32),
            pltpu.VMEM((local, rows), F32),
            pltpu.VMEM((rows, local), F32),
        ]
        + [
            dma((BUFFERS,)),
            dma((9,)),
            dma((n, 2, 2)),
            dma((n, 2)),
            dma((n, 2)),
            dma((ndp,)),
            dma((ndp,)),
            dma((ndp,)),
            dma((ndp,)),
            dma((ndp,)),
            dma((ndp,)),
            dma((nq, 2)),
            dma((nq, 2)),
            dma((nq, 2, 2)),
            dma((nq, 2, 2)),
            dma((nq, 2, 2)),
            dma((4,)),
            dma((4,)),
            dma((n,)),
            dma((n,)),
        ],
        compiler_params=pltpu.CompilerParams(
            collective_id=0, has_side_effects=True, vmem_limit_bytes=54 * 1024 * 1024
        ),
    )(
        tenant_slot_index, live_row_count, inputs, gain, cotangent, tenant.reshape(1, rows),
        down_row_factor, up_column_factor, down, up, weight,
    )

    shapes = (
        ((rows, local), BF16),
        ((local, rows), BF16),
        ((owned, rank, local), F32),
        ((owned, rank, local), F32),
        ((owned, local), F32),
        ((owned, rank), F32),
        ((owned, rank), F32),
        ((owned, local), F32),
    )
    outs = pl.pallas_call(
        functools.partial(finish, rank, owned, width),
        out_shape=tuple(jax.ShapeDtypeStruct(*r) for r in shapes),
        in_specs=[vmem] * 9,
        out_specs=(anywhere,) * 8,
        scratch_shapes=[
            pltpu.VMEM((owned, rank, local), F32),
            pltpu.VMEM((owned, rank, local), F32),
            pltpu.VMEM((owned, rank), F32),
            pltpu.VMEM((owned, rank), F32),
            dma((6,)),
            dma((2, owned)),
        ],
        compiler_params=pltpu.CompilerParams(vmem_limit_bytes=16 * 1024 * 1024),
    )(projected, grad_t, ga, gb, row_a, col_b, stats, down_column_factor, up_row_factor)
    return outs[:2] + (jnp.swapaxes(outs[2], 1, 2),) + outs[3:]


def solution(mesh):
    return jax.shard_map(
        functools.partial(on_device, mesh.shape["dp"], mesh.shape["fsdp"]),
        mesh=mesh,
        in_specs=(
            P("dp", "fsdp"),
            P("fsdp"),
            P(None, "fsdp"),
            P("fsdp", None, None),
            P(None, None, "fsdp"),
            P("dp"),
            P(),
            P("dp"),
            P("dp", "fsdp"),
            P("dp", "fsdp"),
            P("dp", None),
            P("dp", None),
            P("dp", "fsdp"),
        ),
        out_specs=(
            P("dp", "fsdp"),
            P("fsdp", "dp"),
            P("dp", "fsdp", None),
            P("dp", None, "fsdp"),
            P("dp", "fsdp"),
            P("dp", None),
            P("dp", None),
            P("dp", "fsdp"),
        ),
        check_vma=False,
    )
```

```python
import functools

import jax
import jax.numpy as jnp
from jax import lax
from jax.experimental import pallas as pl
from jax.experimental.pallas import tpu as pltpu
from jax.sharding import PartitionSpec as P

ADAPTER_SCALE = 0.5
BETA_TWO = 0.9
SQ_EPS = 1e-30
RMS_EPS = 1e-05
BUFFERS = 5
LANES = 128
TILES_PER_PIECE = 80
LEAD = 2.5
SHARED_COST = 1.7
NT = (((1,), (1,)), ((), ()))
TN = (((0,), (0,)), ((), ()))
F32, BF16 = jnp.float32, jnp.bfloat16
MESH = pl.DeviceIdType.MESH


def xor(a, b, count):
    out, bit = 0, 1
    while bit < count:
        out = out + ((a // bit + b // bit) % 2) * bit
        bit *= 2
    return out


def kernel(
    ndp, n, rank, tenants, owned, width,
    slots, live, x_hbm, gain_hbm, cot_hbm, tenant_hbm, drf_hbm, ucf_hbm, down_hbm, up_hbm, weight,
    projected, grad_t, ga, gb, row_a, col_b, stats,
    wbuf, ag, dpx, dpg, grad, gradt, acc, part, psend, prx, csend, uprx, dnrx,
    xin, cot, gain, tenant, drf, ucf, down, up,
    pk, pkm, pkh, pksu, pksd, pku, pkd, pkt, sm, smrx, st, strx, spread_a, spread_b, lanes, scale_col, base, adapted,
    wsem, in_s, ag_s, ag_sp, ag_r, dx_s, dx_r, dg_s, dg_r, sm_s, sm_r, pp_s, pp_r, ch_s, up_r, dn_r,
    pk_s, pk_r, st_s, st_r,
):
    rows, local = xin.shape
    tile = local // 2
    nq = n // 2
    shared = min(2, nq)
    first, count = 4 * (nq - shared), 4 * nq
    total = count + first
    d = lax.axis_index("dp")
    f = lax.axis_index("fsdp")
    q, c = f // 2, f % 2
    mate = 2 * q + 1 - c

    def remote(src, dst, ssem, rsem, **where):
        return pltpu.make_async_remote_copy(
            src_ref=src, dst_ref=dst, send_sem=ssem, recv_sem=rsem,
            device_id=where, device_id_type=MESH,
        )

    def order(s):
        low = q < nq // 2
        at = jnp.where(low, q, nq - 1 - q)
        t = jnp.where(s < nq - 1 - at, nq - 1 - s, s - (nq - 1 - at))
        return jnp.where(low, t, nq - 1 - t)

    def block(i):
        back = i < count
        i2 = jnp.where(back, i, i - count)
        r = i2 % 4
        t = order(jnp.where(back, i2 // 4, nq - shared - 1 - i2 // 4))
        half, p = r % 2, r // 2
        core = jnp.where(back, (1 - c) * (1 - half) + c * half, c * (1 - half) + (1 - c) * half)
        return t, half, p, core

    def start_row(i):
        t, _, p, core = block(i)
        return (2 * t + core) * local + p * tile

    def load(i):
        return pltpu.make_async_copy(
            weight.at[pl.ds(pl.multiple_of(start_row(i), tile), tile), :],
            wbuf.at[i % BUFFERS], wsem.at[i % BUFFERS],
        )

    ins = [
        pltpu.make_async_copy(a, b, in_s.at[k])
        for k, (a, b) in enumerate(
            (
                (gain_hbm, gain), (x_hbm.at[:, 0:tile], xin.at[:, 0:tile]),
                (x_hbm.at[:, tile:local], xin.at[:, tile:local]), (cot_hbm, cot), (tenant_hbm, tenant),
                (down_hbm, down), (up_hbm, up), (drf_hbm, drf), (ucf_hbm, ucf),
            )
        )
    ]
    for k in range(7):
        ins[k].start()
    for i in range(BUFFERS):
        load(jnp.int32(i)).start()
    for k in range(7, 9):
        ins[k].start()

    barrier = pltpu.get_barrier_semaphore()

    def greet(**where):
        pl.semaphore_signal(barrier, inc=1, device_id=where, device_id_type=MESH)

    for k in range(1, ndp):
        greet(dp=(d + k) % ndp)
    greet(fsdp=mate)

    @pl.when(q + 1 < nq)
    def _():
        greet(fsdp=(f + 2) % n)

    @pl.when(q > 0)
    def _():
        greet(fsdp=(f + n - 2) % n)

    def ag_up(slot, p):
        return remote(ag.at[slot, p], ag.at[slot, p], ag_s.at[slot, p, 0], ag_r.at[slot, p], fsdp=(f + 2) % n)

    def ag_down(slot, p):
        return remote(ag.at[slot, p], ag.at[slot, p], ag_s.at[slot, p, 1], ag_r.at[slot, p], fsdp=(f + n - 2) % n)

    def ag_mate(slot, p):
        return remote(ag.at[slot, p], ag.at[slot, p], ag_sp.at[slot, p], ag_r.at[slot, p], fsdp=mate)

    def ag_own(p):
        @pl.when(q + 1 < nq)
        def _():
            ag_up(f, p).start()

        @pl.when(q > 0)
        def _():
            ag_down(f, p).start()

        ag_mate(f, p).start()

    def prepare(p, square):
        for j in range(p * tile // LANES, (p + 1) * tile // LANES):
            cols = slice(j * LANES, (j + 1) * LANES)
            xf = xin[:, cols].astype(F32)
            gained = (xf * gain[j : j + 1, :].astype(F32)).astype(BF16)
            square = square + xf * xf
            dpx[d, :, cols] = gained
            ag[f, p, :, j * LANES - p * tile : (j + 1) * LANES - p * tile] = gained
        return square

    ins[0].wait()
    ins[1].wait()
    square = prepare(0, jnp.zeros((rows, LANES), F32))
    pl.semaphore_wait(barrier, ndp + (q + 1 < nq).astype(jnp.int32) + (q > 0).astype(jnp.int32))
    ag_own(0)
    ins[2].wait()
    square = prepare(1, square)

    near, far = xor(d, 1, ndp), xor(d, 2, ndp)
    relayed = ndp == 4

    def dp_x(slot, to, k):
        return remote(dpx.at[slot], dpx.at[slot], dx_s.at[k], dx_r.at[slot], dp=to)

    def dp_g(slot, to, k):
        return remote(dpg.at[slot], dpg.at[slot], dg_s.at[k], dg_r.at[slot], dp=to)

    if relayed:
        dp_x(d, near, 0).start()
    ins[3].wait()
    ins[4].wait()
    alive = lax.broadcasted_iota(jnp.int32, (rows, LANES), 0) < live[0]
    for j in range(local // LANES):
        cols = slice(j * LANES, (j + 1) * LANES)
        kept = jnp.where(alive, cot[:, cols].astype(F32), 0.0)
        gradt[cols, :] = kept.T.astype(BF16)
        kept = kept.astype(BF16)
        grad[:, cols] = kept
        dpg[d, :, cols] = kept
    if relayed:
        dp_g(d, far, 0).start()
        dp_g(d, near, 1).start()
        dp_x(d, far, 1).start()
    else:
        for k in range(1, ndp):
            dp_x(d, (d + k) % ndp, k - 1).start()
            dp_g(d, (d + k) % ndp, k - 1).start()

    def relay():
        dp_x(near, far, 2).wait_recv()
        dp_x(near, far, 2).start()
        dp_g(far, near, 2).wait_recv()
        dp_g(far, near, 2).start()

    place_of = lax.broadcasted_iota(jnp.int32, (tenants * rank, rows), 0) // rank
    tenant_row = tenant[...]
    picked = place_of == tenant_row
    ins[5].wait()
    ins[6].wait()
    for at, lhs, rhs in ((0, down, dpx.at[d]), (1, up, grad)):
        full = lax.dot_general(lhs[...], rhs[...], NT, preferred_element_type=F32)
        full = jnp.where(picked, full, 0.0).reshape(tenants, rank, rows)
        pk[at, 0:rank, :] = jnp.sum(full, axis=0)
    power = jnp.sum(square.T, axis=0, keepdims=True)
    pk[0, rank : rank + 8, :] = jnp.broadcast_to(power, (8, rows))
    pk[1, rank : rank + 8, :] = jnp.zeros((8, rows), F32)

    pk_mate = remote(pk.at[1 - c], pkm, pk_s.at[0], pk_r.at[0], fsdp=mate)
    pk_mate.start()

    def pk_up():
        return remote(pksu, pku, pk_s.at[1], pk_r.at[1], fsdp=(f + 2) % n)

    def pk_down():
        return remote(pksd, pkd, pk_s.at[2], pk_r.at[2], fsdp=(f + n - 2) % n)

    def pk_back():
        return remote(pkt.at[c], pkt.at[c], pk_s.at[3], pk_r.at[3], fsdp=mate)

    def pk_spread():
        pk_mate.wait_recv()
        pkh[...] = pk[c] + pkm[...]

        @pl.when(q == 0)
        def _():
            pksu[...] = pkh[...]
            pk_up().start()

        @pl.when(q == nq - 1)
        def _():
            pksd[...] = pkh[...]
            pk_down().start()

    def pk_hop(j):
        @pl.when((q == j) & (q + 1 < nq))
        def _():
            pk_up().wait_recv()
            pksu[...] = pkh[...] + pku[...]
            pk_up().start()

        @pl.when((nq - 1 - q == j) & (q > 0))
        def _():
            pk_down().wait_recv()
            pksd[...] = pkh[...] + pkd[...]
            pk_down().start()

    def pk_sum():
        @pl.when(q == nq - 1)
        def _():
            pk_up().wait_recv()

        @pl.when(q == 0)
        def _():
            pk_down().wait_recv()

        below = jnp.where(q > 0, pku[...], 0.0)
        above = jnp.where(q + 1 < nq, pkd[...], 0.0)
        pkt[c] = pkh[...] + below + above
        pk_back().start()

    def sm_copy(k):
        return remote(sm, smrx.at[d], sm_s.at[k], sm_r.at[k], dp=(d + k) % ndp)

    def pk_use():
        pk_back().wait_recv()
        scale = lax.rsqrt(pkt[0, rank : rank + 1, :] / width + RMS_EPS)
        inner = pkt[0, 0:rank, :] * scale
        back = pkt[1, 0:rank, :]
        slot = jnp.zeros((1, rows), F32)
        for t in range(tenants):
            slot = jnp.where(tenant_row == t, slots[t].astype(F32), slot)
        sm[0:rank, :] = inner.astype(BF16)
        sm[rank : 2 * rank, :] = (back * scale).astype(BF16)
        sm[2 * rank :, :] = jnp.broadcast_to(slot, (16, rows)).astype(BF16)
        for k in range(1, ndp):
            sm_copy(k).start()
        smrx[d] = sm[...]
        spread_a[...] = jnp.where(picked, jnp.tile(inner, (tenants, 1)), 0.0).astype(BF16)
        spread_b[...] = jnp.where(picked, jnp.tile(back, (tenants, 1)), 0.0).astype(BF16)
        scale_col[...] = jnp.broadcast_to(scale, (rows, rows)).T

    def chain_copy(t, p, h, rsem, rx, to):
        part_of = pl.ds(h * (tile // 2), tile // 2)
        return remote(
            csend.at[t, p, part_of], rx.at[t, p, part_of], ch_s.at[t, p, h], rsem.at[t, p, h], fsdp=to
        )

    def chain_up(t, p, h):
        return chain_copy(t, p, h, up_r, uprx, (f + 2) % n)

    def chain_down(t, p, h):
        return chain_copy(t, p, h, dn_r, dnrx, (f + n - 2) % n)

    def send_up(t, p):
        chain_up(t, p, 0).start()

        @pl.when((t != q + 1) | (p == 0))
        def _():
            chain_up(t, p, 1).start()

    def send_down(t, p):
        chain_down(t, p, 0).start()

        @pl.when((t != q - 1) | (p == 0))
        def _():
            chain_down(t, p, 1).start()

    def mate_copy(t, p):
        return remote(psend.at[t, p], prx.at[t, p], pp_s.at[t, p], pp_r.at[t, p], fsdp=mate)

    def both(t, p):
        return part[t, p].astype(F32) + prx[t, p].astype(F32)

    def head(t):
        return ((t > q) & (q == 0)) | ((t < q) & (q == nq - 1))

    def chain_head(t, p):
        mate_copy(t, p).wait_recv()
        csend[t, p] = both(t, p).astype(BF16)

        @pl.when(t > q)
        def _():
            send_up(t, p)

        @pl.when(t < q)
        def _():
            send_down(t, p)

    def tick(j):
        k, p = (j + 1) // 2, (j + 1) % 2
        below, above = 2 * (q - k) + c, 2 * (q + k) + c
        pk_hop(j)

        m = j - 1 - 2 * q

        @pl.when((q > 0) & (m >= 0) & (m < 2 * (nq - 1 - q)))
        def _():
            t, b = nq - 1 - m // 2, m % 2
            mate_copy(t, b).wait_recv()
            for h in range(2):
                chain_up(t, b, h).wait_recv()
            csend[t, b] = (both(t, b) + uprx[t, b].astype(F32)).astype(BF16)
            send_up(t, b)

        w = j - 1 - 2 * (nq - 1 - q)

        @pl.when((q < nq - 1) & (w >= 0) & (w < 2 * q))
        def _():
            t, b = w // 2, w % 2
            mate_copy(t, b).wait_recv()
            for h in range(2):
                chain_down(t, b, h).wait_recv()
            csend[t, b] = (both(t, b) + dnrx[t, b].astype(F32)).astype(BF16)
            send_down(t, b)

        @pl.when(q - k >= 0)
        def _():
            ag_up(below, p).wait_recv()

            @pl.when(q + 1 < nq)
            def _():
                ag_up(below, p).start()

            ag_mate(below, p).start()

        @pl.when(q + k < nq)
        def _():
            ag_down(above, p).wait_recv()

            @pl.when(q > 0)
            def _():
                ag_down(above, p).start()

            ag_mate(above, p).start()

    def adapter_base():
        chunk = min(512, local)
        for lo in range(0, local, chunk):
            here = slice(lo, lo + chunk)
            adapted[:, here] = ADAPTER_SCALE * lax.dot_general(
                spread_a[...], up[:, here], TN, preferred_element_type=F32
            )

    def gradient_base():
        for p in range(2):
            mate_copy(q, p).wait_recv()
            for h in range(2):
                here = slice(h * quarter, (h + 1) * quarter)
                there = slice(p * tile + h * quarter, p * tile + (h + 1) * quarter)
                out = lax.dot_general(down[:, there], spread_b[...], TN, preferred_element_type=F32)
                out = ADAPTER_SCALE * out + part[q, p, here, :].astype(F32) + prx[q, p, here, :].astype(F32)
                base[there, :] = out

    quarter = tile // 2
    period = max(TILES_PER_PIECE * rows // local, 3)
    ticks = 2 * (nq - 1)
    spent, at, when = 0.0, 0, []
    for j in range(1, ticks + 1):
        while spent < period * j - LEAD and at < total:
            spent += SHARED_COST if first <= at < count else 1.0
            at += 1
        when.append(at)
    for j in range(ticks, 0, -1):
        needed = count + 2 * j - 6 if j > 2 else count + 2 * j - 10
        later = when[j] - 1 if j < ticks else total - 1
        when[j - 1] = max(min(when[j - 1], needed, later), 2 * j)
    chained = when[nq - 2]
    once = [(2, pk_spread), (2, lambda: ag_own(1)), (chained + 2, pk_sum), (chained + 4, pk_use)]
    once += [(total - 4, adapter_base), (total - 3, gradient_base)]
    if relayed:
        once.append((first + 2, relay))

    def events(i, lo, hi):
        for at, what in once:
            if lo <= at < hi:
                pl.when(i == at)(what)
        j = jnp.int32(0)
        for k, at in enumerate(when):
            if lo <= at < hi:
                j = jnp.where(i == at, k + 1, j)
        if any(lo <= at < hi for at in when):
            pl.when(j > 0)(lambda: tick(j))

    def backward(i):
        t, half, p, _ = block(i)
        out = jnp.dot(wbuf[i % BUFFERS], gradt[...], preferred_element_type=F32).astype(BF16)

        @pl.when(half == 0)
        def _():
            psend[t, p] = out
            mate_copy(t, p).start()

        @pl.when(half == 1)
        def _():
            part[t, p] = out

        @pl.when((i % 4 == 3) & head(t))
        def _():
            chain_head(t, 0)
            chain_head(t, 1)

    def forward(i):
        t, _, p, core = block(i)
        slot = 2 * t + core

        @pl.when(core != c)
        def _():
            ag_mate(slot, p).wait_recv()

        acc[...] += jnp.dot(ag[slot, p], wbuf[i % BUFFERS], preferred_element_type=F32)

    def refill(i):
        @pl.when(i + BUFFERS < total)
        def _():
            load(i + BUFFERS).start()

    @pl.loop(0, first)
    def _(i):
        events(i, 0, first)
        load(i).wait()
        backward(i)
        refill(i)

    acc[...] = jnp.zeros_like(acc)

    @pl.loop(first, count)
    def _(i):
        events(i, first, count)
        load(i).wait()
        backward(i)

        @pl.when(i >= 0)
        def _():
            forward(i)

        refill(i)

    @pl.loop(count, total)
    def _(i):
        events(i, count, total)
        load(i).wait()
        forward(i)
        refill(i)

    if relayed:
        corner = xor(d, 3, ndp)
        for slot in (far, corner):
            dp_x(slot, far, 0).wait_recv()
        for slot in (near, corner):
            dp_g(slot, near, 0).wait_recv()
    else:
        for k in range(1, ndp):
            dp_x((d + k) % ndp, (d + 1) % ndp, 0).wait_recv()
            dp_g((d + k) % ndp, (d + 1) % ndp, 0).wait_recv()
    for k in range(1, ndp):
        sm_copy(k).wait_recv()
    ins[7].wait()
    ins[8].wait()
    place = lax.broadcasted_iota(jnp.int32, (owned * rank, rows), 0) // rank + d * owned
    place = place.astype(F32)
    for at, src, dst, summed, old, line in (
        (rank, dpx, ga, row_a, drf, 0), (0, dpg, gb, col_b, ucf, owned * rank)
    ):
        lhs = jnp.concatenate(
            [
                jnp.where(
                    place == smrx[g, 2 * rank : 2 * rank + 1, :].astype(F32),
                    jnp.tile(smrx[g, at : at + rank, :].astype(F32), (owned, 1)),
                    0.0,
                ).astype(BF16)
                for g in range(ndp)
            ],
            axis=1,
        )
        step = min(512, local)
        for lo in range(0, local, step):
            rhs = src[:, :, lo : lo + step].reshape(ndp * rows, step)
            full = ADAPTER_SCALE * jnp.dot(lhs, rhs, preferred_element_type=F32)
            full = full.reshape(owned, rank, step)
            dst[:, :, lo : lo + step] = full
            sq = full * full + SQ_EPS
            summed[:, lo : lo + step] = BETA_TWO * old[:, lo : lo + step] + (1.0 - BETA_TWO) * (
                jnp.sum(sq, axis=1) / rank
            )
            flat = sq.reshape(owned * rank, step)
            summed_up = flat[:, 0:LANES]
            for w in range(LANES, step, LANES):
                summed_up = summed_up + flat[:, w : w + LANES]
            here = slice(line, line + owned * rank)
            if lo == 0:
                lanes[here, :] = summed_up
            else:
                lanes[here, :] += summed_up
    cols = 2 * owned * rank
    st[...] = jnp.zeros_like(st)
    factor = drf[:, 0:LANES]
    for w in range(LANES, local, LANES):
        factor = factor + drf[:, w : w + LANES]
    lanes[cols:, :] = jnp.concatenate([factor, jnp.zeros((LANES - owned, LANES), F32)], axis=0)
    for k in range(cols // LANES + 1):
        st[k : k + 1, :] = jnp.sum(lanes[k * LANES : (k + 1) * LANES, :].T, axis=0, keepdims=True)

    def st_copy(k):
        return remote(st, strx.at[k], st_s.at[k], st_r.at[k], fsdp=(f + k) % n)

    for k in range(1, n):
        st_copy(k).start()

    @pl.when(q + 1 < nq)
    def _():
        chain_up(q + 1, 1, 1).start()

    @pl.when(q > 0)
    def _():
        chain_down(q - 1, 1, 1).start()
    wide = jnp.concatenate([scale_col[...]] * (local // rows), axis=1)
    projected[...] = (acc[...] * wide + adapted[...]).astype(BF16)
    for p in range(2):
        for h in range(2):
            here = slice(h * quarter, (h + 1) * quarter)
            there = slice(p * tile + h * quarter, p * tile + (h + 1) * quarter)

            @pl.when(q > 0)
            def _():
                chain_up(q, p, h).wait_recv()

            @pl.when(q < nq - 1)
            def _():
                chain_down(q, p, h).wait_recv()

            from_up = jnp.where(q > 0, uprx[q, p, here, :].astype(F32), 0.0)
            from_dn = jnp.where(q < nq - 1, dnrx[q, p, here, :].astype(F32), 0.0)
            grad_t[there, :] = (base[there, :] + from_up + from_dn).astype(BF16)

    whole = st[...]
    for k in range(1, n):
        st_copy(k).wait_recv()
        whole = whole + strx[k]
    stats[...] = whole
    pk_mate.wait_send()
    pk_back().wait_send()

    @pl.when(q + 1 < nq)
    def _():
        pk_up().wait_send()

    @pl.when(q > 0)
    def _():
        pk_down().wait_send()

    for k in range(1, n):
        st_copy(k).wait_send()
    for k in range(1, ndp):
        sm_copy(k).wait_send()
        dp_x(d, (d + 1) % ndp, k - 1).wait_send()
        dp_g(d, (d + 1) % ndp, k - 1).wait_send()

    @pl.loop(0, nq)
    def _(t):
        slot = 2 * t + c
        for p in range(2):
            mate_copy(t, p).wait_send()

            @pl.when(t != q)
            def _():
                for h in range(2):
                    chain_up(t, p, h).wait_send()

            ag_mate(slot, p).wait_send()

            @pl.when((t <= q) & (q + 1 < nq))
            def _():
                ag_up(slot, p).wait_send()

            @pl.when((t >= q) & (q > 0))
            def _():
                ag_down(slot, p).wait_send()


def finish(
    rank, owned, width,
    projected, grad_t, ga, gb, row_a, col_b, stats, dcf, urf,
    projected_out, grad_t_out, update_a_out, update_b_out, row_a_out, col_a_out, row_b_out, col_b_out,
    update_a, update_b, col_a, row_b, sems, slot_sems,
):
    copies = [
        pltpu.make_async_copy(src, dst, sems.at[k])
        for k, (src, dst) in enumerate(
            (
                (projected, projected_out), (grad_t, grad_t_out), (row_a, row_a_out), (col_b, col_b_out),
                (col_a, col_a_out), (row_b, row_b_out),
            )
        )
    ]
    for k in range(4):
        copies[k].start()
    per = LANES // rank
    lines = owned // per
    sums = [
        jnp.concatenate(
            [
                stats[base + s // per : base + s // per + 1, s % per * rank : (s % per + 1) * rank]
                for s in range(owned)
            ],
            axis=0,
        )
        for base in (0, lines)
    ]
    new_a = BETA_TWO * dcf[...] + (1.0 - BETA_TWO) * (sums[0] / width)
    new_b = BETA_TWO * urf[...] + (1.0 - BETA_TWO) * (sums[1] / width)
    col_a[...] = new_a
    row_b[...] = new_b
    for k in (4, 5):
        copies[k].start()
    line = jnp.broadcast_to(stats[2 * lines : 2 * lines + 1, :], (owned, LANES))
    own = lax.broadcasted_iota(jnp.int32, (owned, LANES), 0) == lax.broadcasted_iota(
        jnp.int32, (owned, LANES), 1
    )
    kept = jnp.sum(jnp.where(own, line, 0.0), axis=1, keepdims=True)
    mean_a = (BETA_TWO * kept + (1.0 - BETA_TWO) * (jnp.sum(sums[0], axis=1, keepdims=True) / rank)) / width
    mean_b = jnp.sum(new_b, axis=1, keepdims=True) / rank
    wide_a = lax.rsqrt(row_a[...] / mean_a)
    wide_b = lax.rsqrt(col_b[...])
    tall_a = lax.rsqrt(new_a).T
    tall_b = lax.rsqrt(new_b / mean_b).T
    work = ((ga, update_a, update_a_out, wide_a, tall_a), (gb, update_b, update_b_out, wide_b, tall_b))
    for s in range(owned):
        for which, (src, dst, out, wide, tall) in enumerate(work):
            dst[s] = src[s] * wide[s : s + 1, :] * tall[:, s : s + 1]
            copy = pltpu.make_async_copy(dst.at[s], out.at[s], slot_sems.at[which, s])
            copy.start()
            copies.append(copy)
    for copy in copies:
        copy.wait()


def on_device(
    ndp,
    n,
    inputs,
    norm_gain_vector,
    weight,
    down_adapters,
    up_adapters,
    tenant,
    tenant_slot_index,
    live_row_count,
    cotangent,
    down_row_factor,
    down_column_factor,
    up_row_factor,
    up_column_factor,
):
    rows, local = inputs.shape
    width = weight.shape[0]
    tenants, rank = down_adapters.shape[1:]
    owned = down_row_factor.shape[0]
    down = jnp.transpose(down_adapters, (1, 2, 0)).reshape(tenants * rank, local)
    up = up_adapters.reshape(tenants * rank, local)
    gain = norm_gain_vector.reshape(local // LANES, LANES)
    tile = local // 2
    nq = n // 2
    cols = 2 * owned * rank
    dma = pltpu.SemaphoreType.DMA
    piece = pltpu.VMEM((nq, 2, tile, rows), BF16)
    anywhere = pl.BlockSpec(memory_space=pl.ANY)
    vmem = pl.BlockSpec(memory_space=pltpu.VMEM)
    scalar = pl.BlockSpec(memory_space=pltpu.SMEM)
    small = pltpu.VMEM((rank + 8, rows), F32)
    results = (
        ((rows, local), BF16),
        ((local, rows), BF16),
        ((owned, rank, local), F32),
        ((owned, rank, local), F32),
        ((owned, local), F32),
        ((owned, local), F32),
        ((8, LANES), F32),
    )
    projected, grad_t, ga, gb, row_a, col_b, stats = pl.pallas_call(
        functools.partial(kernel, ndp, n, rank, tenants, owned, width),
        out_shape=tuple(pltpu.VMEM(*r) for r in results),
        in_specs=[scalar] * 2 + [anywhere] * 9,
        out_specs=(vmem,) * 7,
        scratch_shapes=[
            pltpu.VMEM((BUFFERS, tile, local), BF16),
            pltpu.VMEM((n, 2, rows, tile), BF16),
            pltpu.VMEM((ndp, rows, local), BF16),
            pltpu.VMEM((ndp, rows, local), BF16),
            pltpu.VMEM((rows, local), BF16),
            pltpu.VMEM((local, rows), BF16),
            pltpu.VMEM((rows, local), F32),
            piece, piece, piece, piece, piece, piece,
            pltpu.VMEM((rows, local), BF16),
            pltpu.VMEM((rows, local), BF16),
            pltpu.VMEM((local // LANES, LANES), BF16),
            pltpu.VMEM((1, rows), jnp.int32),
            pltpu.VMEM((owned, local), F32),
            pltpu.VMEM((owned, local), F32),
            pltpu.VMEM((tenants * rank, local), BF16),
            pltpu.VMEM((tenants * rank, local), BF16),
            pltpu.VMEM((2, rank + 8, rows), F32),
            small, small, small, small, small, small,
            pltpu.VMEM((2, rank + 8, rows), F32),
            pltpu.VMEM((2 * rank + 16, rows), BF16),
            pltpu.VMEM((ndp, 2 * rank + 16, rows), BF16),
            pltpu.VMEM((8, LANES), F32),
            pltpu.VMEM((n, 8, LANES), F32),
            pltpu.VMEM((tenants * rank, rows), BF16),
            pltpu.VMEM((tenants * rank, rows), BF16),
            pltpu.VMEM((cols + LANES, LANES), F32),
            pltpu.VMEM((rows, rows), F32),
            pltpu.VMEM((local, rows), F32),
            pltpu.VMEM((rows, local), F32),
        ]
        + [
            dma((BUFFERS,)),
            dma((9,)),
            dma((n, 2, 2)),
            dma((n, 2)),
            dma((n, 2)),
            dma((ndp,)),
            dma((ndp,)),
            dma((ndp,)),
            dma((ndp,)),
            dma((ndp,)),
            dma((ndp,)),
            dma((nq, 2)),
            dma((nq, 2)),
            dma((nq, 2, 2)),
            dma((nq, 2, 2)),
            dma((nq, 2, 2)),
            dma((4,)),
            dma((4,)),
            dma((n,)),
            dma((n,)),
        ],
        compiler_params=pltpu.CompilerParams(
            collective_id=0, has_side_effects=True, vmem_limit_bytes=54 * 1024 * 1024
        ),
    )(
        tenant_slot_index, live_row_count, inputs, gain, cotangent, tenant.reshape(1, rows),
        down_row_factor, up_column_factor, down, up, weight,
    )

    shapes = (
        ((rows, local), BF16),
        ((local, rows), BF16),
        ((owned, rank, local), F32),
        ((owned, rank, local), F32),
        ((owned, local), F32),
        ((owned, rank), F32),
        ((owned, rank), F32),
        ((owned, local), F32),
    )
    outs = pl.pallas_call(
        functools.partial(finish, rank, owned, width),
        out_shape=tuple(jax.ShapeDtypeStruct(*r) for r in shapes),
        in_specs=[vmem] * 9,
        out_specs=(anywhere,) * 8,
        scratch_shapes=[
            pltpu.VMEM((owned, rank, local), F32),
            pltpu.VMEM((owned, rank, local), F32),
            pltpu.VMEM((owned, rank), F32),
            pltpu.VMEM((owned, rank), F32),
            dma((6,)),
            dma((2, owned)),
        ],
        compiler_params=pltpu.CompilerParams(vmem_limit_bytes=16 * 1024 * 1024),
    )(projected, grad_t, ga, gb, row_a, col_b, stats, down_column_factor, up_row_factor)
    return outs[:2] + (jnp.swapaxes(outs[2], 1, 2),) + outs[3:]


def solution(mesh):
    return jax.shard_map(
        functools.partial(on_device, mesh.shape["dp"], mesh.shape["fsdp"]),
        mesh=mesh,
        in_specs=(
            P("dp", "fsdp"),
            P("fsdp"),
            P(None, "fsdp"),
            P("fsdp", None, None),
            P(None, None, "fsdp"),
            P("dp"),
            P(),
            P("dp"),
            P("dp", "fsdp"),
            P("dp", "fsdp"),
            P("dp", None),
            P("dp", None),
            P("dp", "fsdp"),
        ),
        out_specs=(
            P("dp", "fsdp"),
            P("fsdp", "dp"),
            P("dp", "fsdp", None),
            P("dp", None, "fsdp"),
            P("dp", "fsdp"),
            P("dp", None),
            P("dp", None),
            P("dp", "fsdp"),
        ),
        check_vma=False,
    )
```
